256 devices in a mesh: tile: 64 (over y, z, core), sec: 4 (over x).
Axes of the slice: x: 4, y: 4, z: 8, core: 2. Of those that a mesh axis runs over, the one named last changes fastest.
Arguments:
- voltage: float32 [8192, 512], P('tile', 'sec'), may hold values from -6 to 6
- conductance: float32 [8192, 512], P('tile', 'sec'), may hold values from 0.2 to 2
- reversal: float32 [8192, 512], P('tile', 'sec'), may hold values from -1 to 1
- drive: bfloat16 [8, 8192, 512], P(None, 'tile', 'sec'), may hold values from -6 to 6
- inv_cable: float32 [128, 128], replicated, may hold values from -1 to 1
- owner_map: int32 [8192], P('tile'), may hold values from 0 to 63, as said below
- peer_counts: int32 [64, 64], P('tile'), may hold values from 0 to 4, as said below
- pattern: int32 [4, 8192, 2], P('sec', 'tile'), may hold values from 0 to 31, all different within a row
- transfer: bfloat16 [4, 8192, 2, 128, 128], P('sec', 'tile'), may hold values from -0.01171875 to 0.01171875
Outputs:
- final_voltage: float32 [8192, 512], P('tile', 'sec')
- probe: float32 [8, 4096], P(None, ('tile', 'sec'))
The draws below stay inside these ranges and needn't reach their ends.
Inputs may be any that keep to these rules, and one draw needn't show every extreme that they name: `owner_map`: every depth tile owns exactly 128 cells; the cells c with c // 128 = u include at most 4 cells of one owner, and exactly 4 of some owner. peer_counts[d, u] is the number of cells c with c // 128 = u and owner_map[c] = d. `pattern`: the 2 contact tiles of one slot and section differ.
All inputs are finite; a program needn't handle non-finite values.
Results may differ from the reference program's by a relative error of at most 0.0029.
Values may be sent and summed in bfloat16 or wider, within the bound.
A program may use at most 64 MiB of HBM per device.

```python
import math
import jax
import jax.numpy as jnp
from jax import lax

SEG = 128
CW = 128
CONTACTS = 4096
KB = 2
CELL_DEV = 128
STEPS = 8
OWNERS = 64
SECTIONS = 4
CELLS = 8192
COMPS = 512
CAP = 4
N_TILE = 64
N_SEC = 4


def tile_layout(key):
    base_key = jax.random.fold_in(key, 11)
    load_key, perm_key, shuffle_key = jax.random.split(base_key, 3)
    half_count = OWNERS // 2
    chosen = jax.random.randint(load_key, (half_count,), 0, CAP + 1).astype(jnp.int32)
    chosen = chosen.at[0].set(CAP)
    peer_loads = jnp.concatenate([chosen, CAP - chosen])
    peer_loads = peer_loads[jax.random.permutation(perm_key, OWNERS)]
    owners = jnp.arange(OWNERS, dtype=jnp.int32)
    counts = peer_loads[(owners[:, None] - owners[None, :]) % OWNERS]
    bounds = jnp.cumsum(counts, axis=0)
    places = jnp.arange(CELL_DEV, dtype=jnp.int32)
    owner_pos = jnp.sum((bounds.T[:, None, :] <= places[None, :, None]).astype(jnp.int32), axis=2)
    orders = jax.vmap(lambda one_key: jax.random.permutation(one_key, CELL_DEV))(jax.random.split(shuffle_key, OWNERS))
    owner_map = jnp.take_along_axis(owner_pos, orders, axis=1).reshape(-1)
    return (owner_map.astype(jnp.int32), counts.astype(jnp.int32))


def draw_owner_map(key, part):
    return tile_layout(key)[0]


def draw_peer_counts(key, part):
    return tile_layout(key)[1]


def draw_inv_cable(key, part):
    first_key, second_key = jax.random.split(jax.random.fold_in(key, 5))
    diagonal = jax.random.uniform(first_key, (SEG,), jnp.float32, 0.4, 0.6)
    spread = jnp.clip(jax.random.normal(second_key, (SEG, SEG), jnp.float32), -4.0, 4.0) * (0.2 / math.sqrt(SEG))
    return spread + jnp.eye(SEG, dtype=jnp.float32) * diagonal[None, :]


def shard_levels(own_key, shape, shards, smallest, top_value):
    factor_of, own = 1.0, jax.random.fold_in(own_key, 6)
    for dim, shards_of in shards:
        draws = jnp.exp(jax.random.uniform(jax.random.fold_in(own, dim), (shards_of,), jnp.float32, smallest / len(shards), top_value / len(shards)))
        factor_of = factor_of * jnp.repeat(draws, shape[dim] // shards_of).reshape([-1 if axis == dim else 1 for axis in range(len(shape))])
    return factor_of


def choose_distinct(stream_key, rows, count, top, lift):
    order = jax.random.permutation(jax.random.fold_in(stream_key, 1), count)
    boost = order
    for power in range(3):
        boost = boost * boost // count
    boost = boost * lift // count
    chance = jax.random.randint(jax.random.fold_in(stream_key, 2), (rows, count), 0, 4096) + boost
    holders = jax.random.permutation(jax.random.fold_in(stream_key, 3), rows)[jnp.arange(count) % rows]
    chance = jnp.where(jnp.arange(rows)[:, None] == holders[None, :], 1 << 14, chance)
    priority = chance * count + jnp.arange(count)
    return lax.top_k(priority.astype(jnp.int32), top)[1].astype(jnp.int32)


def normal_values(own_key, extent, width, most, cuts=(), kind=jnp.bfloat16):
    drawn = width * jax.random.normal(own_key, extent, jnp.float32)
    if cuts:
        drawn = drawn * shard_levels(own_key, extent, cuts, -0.22, 0.18)
    return jnp.clip(drawn, -most, most).astype(kind)


def setup_inputs(seed: int = 0) -> dict:
    seeds = jax.random.split(jax.random.key(seed), 10)
    return {
        "voltage": normal_values(seeds[0], (CELLS, COMPS), 1.0, 6.0, ((0, 64), (1, 4)), jnp.float32),
        "conductance": jnp.clip(jnp.exp(math.log(2.0) - 2.3025851 * jax.random.uniform(seeds[1], (CELLS, COMPS), jnp.float32) ** shard_levels(seeds[1], (CELLS, COMPS), ((0, 64), (1, 4)), -0.2, 0.2)), 0.2, 2.0),
        "reversal": jnp.clip(jax.random.uniform(seeds[2], (CELLS, COMPS), jnp.float32, -1.0, 1.0) * shard_levels(seeds[2], (CELLS, COMPS), ((0, 64), (1, 4)), -0.4, 0.0), -1.0, 1.0),
        "drive": normal_values(seeds[3], (STEPS, CELLS, COMPS), 1.0, 6.0, ((1, 64), (2, 4))),
        "inv_cable": draw_inv_cable(jax.random.fold_in(seeds[9], 71), 0),
        "owner_map": draw_owner_map(jax.random.fold_in(seeds[9], 71), 0),
        "peer_counts": draw_peer_counts(jax.random.fold_in(seeds[9], 71), 0),
        "pattern": choose_distinct(seeds[7], SECTIONS * CELLS, CONTACTS // CW, KB, 0).reshape((SECTIONS, CELLS, KB)),
        "transfer": normal_values(seeds[8], (SECTIONS, CELLS, KB, SEG, CW), (N_TILE * N_SEC * CELL_DEV * KB * SEG // (CONTACTS // CW)) ** -0.5, 0.01171875, ((0, 4), (1, 64))),
    }


TIME_STEP = 0.25
AXIAL = 2.0


def cable_update(voltage_now, conductance, reversal, drive_now, inv_cable):
    zero_col = jnp.zeros((voltage_now.shape[0], 1), jnp.float32)
    left_end = jnp.concatenate([zero_col, voltage_now[:, :-1, -1]], axis=1)
    right_end = jnp.concatenate([voltage_now[:, 1:, 0], zero_col], axis=1)
    columns = jnp.arange(SEG, dtype=jnp.int32)
    first_col = (columns == 0).astype(jnp.float32)
    last_col = (columns == SEG - 1).astype(jnp.float32)
    boundary = first_col * (left_end[:, :, None] - voltage_now) + last_col * (right_end[:, :, None] - voltage_now)
    driven = drive_now.astype(jnp.float32)
    right_side = voltage_now * (1.0 - TIME_STEP * conductance) + TIME_STEP * (conductance * reversal + driven + AXIAL * boundary)
    voltage_next = jnp.einsum("cni,ji->cnj", right_side, inv_cable, precision=lax.Precision.HIGHEST)
    current = (conductance * (voltage_next - reversal) - driven).astype(jnp.bfloat16)
    return voltage_next, current


def reference(voltage, conductance, reversal, drive, inv_cable, owner_map, peer_counts, pattern, transfer):
    cell_shape = (CELLS, SECTIONS, SEG)
    voltage_now = voltage.reshape(cell_shape)
    cond_cells = conductance.reshape(cell_shape)
    rev_cells = reversal.reshape(cell_shape)
    currents = []
    for step_index in range(STEPS):
        voltage_now, current = cable_update(voltage_now, cond_cells, rev_cells, drive[step_index].reshape(cell_shape), inv_cable)
        currents.append(current)
    current_all = jnp.stack(currents)
    owners = jnp.arange(OWNERS, dtype=jnp.int32)
    member = (owner_map[:, None] == owners[None, :]).astype(jnp.int32)
    running = jnp.cumsum(member.reshape(OWNERS, CELL_DEV, OWNERS), axis=1).reshape(CELLS, OWNERS)
    rank_within = jnp.sum(running * member, axis=1) - 1
    source = jnp.arange(CELLS, dtype=jnp.int32) // CELL_DEV
    starts = jnp.cumsum(peer_counts, axis=1) - peer_counts
    destination = (owner_map * CELL_DEV + starts[owner_map, source] + rank_within).astype(jnp.int32)
    ordered = jnp.zeros_like(current_all).at[:, destination].set(current_all)
    tile_total = CONTACTS // CW
    tile_ids = jnp.arange(tile_total, dtype=jnp.int32)

    def owner_block(probe_sum, owner_index):
        first_row = (owner_index * CELL_DEV).astype(jnp.int32)
        owner_rows = lax.dynamic_slice_in_dim(ordered, first_row, CELL_DEV, 1)
        for section in range(SECTIONS):
            weights = lax.dynamic_slice_in_dim(transfer[section], first_row, CELL_DEV, 0).astype(jnp.float32)
            layout = lax.dynamic_slice_in_dim(pattern[section], first_row, CELL_DEV, 0)
            tile_sums = jnp.einsum("tsi,skic->tskc", owner_rows[:, :, section].astype(jnp.float32), weights, precision=lax.Precision.HIGHEST)
            select = (layout[:, :, None] == tile_ids[None, None, :]).astype(jnp.float32)
            probe_sum = probe_sum + jnp.einsum("tskc,skq->tqc", tile_sums, select, precision=lax.Precision.HIGHEST).reshape(STEPS, CONTACTS)
        return probe_sum, None

    probe_sum, unused_out = lax.scan(owner_block, jnp.zeros((STEPS, CONTACTS), jnp.float32), owners)
    return voltage_now.reshape(CELLS, SECTIONS * SEG), probe_sum
```

```python
import functools

import jax
import jax.numpy as jnp
from jax import lax
from jax.experimental import pallas as pl
from jax.experimental.pallas import tpu as pltpu
from jax.sharding import PartitionSpec as P

MESH = pl.DeviceIdType.MESH
F32 = jnp.float32
BF16 = jnp.bfloat16

STEPS = 8
HALF = 4
CAP = 4
ROWS = CAP * HALF
LAGS = 8
TIME_STEP = 0.25


def far_first(index, count):
    half = lax.div(index + 1, 2)
    return count // 2 + half * (1 - 2 * lax.rem(index, 2))


def split(x):
    high = x.astype(BF16)
    return high, (x - high.astype(F32)).astype(BF16)


def kernel(
    ny,
    nz,
    nsec,
    v_ref,
    g_ref,
    e_ref,
    d_ref,
    a_ref,
    own_ref,
    cnt_ref,
    pat_ref,
    w_hbm,
    fv_ref,
    probe_ref,
    w_ref,
    zs,
    hl,
    hr,
    ends,
    got,
    hpad,
    pick,
    place,
    cur,
    outs,
    recv,
    ordered,
    tiles,
    part,
    first,
    mine,
    second,
    w_sem,
    send_sem,
    recv_sem,
):
    chips = ny * nz
    ntile = 2 * chips
    cells, seg = v_ref.shape
    tile = lax.axis_index("tile")
    sec = lax.axis_index("sec")
    core = lax.rem(tile, 2)
    chip = lax.div(tile, 2)
    my_y = lax.div(chip, nz)
    my_z = lax.rem(chip, nz)
    line = core * nsec + sec

    def chip_at(dy, dz):
        return lax.rem(my_y + dy, ny) * nz + lax.rem(my_z + dz, nz)

    def tile_peer(o):
        pair = lax.rem(o, 2 * ny)
        dz = far_first(lax.div(o, 2 * ny), nz)
        dy = far_first(lax.div(pair, 2), ny)
        return chip_at(dy, dz) * 2 + lax.rem(core + 1 + lax.rem(pair, 2), 2)

    def chip_peer(o):
        return chip_at(far_first(lax.rem(o, ny), ny), far_first(lax.div(o, ny), nz))

    w_copy = pltpu.make_async_copy(w_hbm.at[0], w_ref, w_sem)
    w_copy.start()

    barrier = pltpu.get_barrier_semaphore()

    def greet(o, carry):
        pl.semaphore_signal(
            barrier, inc=1, device_id=(tile_peer(o), sec), device_id_type=MESH
        )
        return carry

    lax.fori_loop(0, ntile - 1, greet, 0)
    for step in range(1, nsec):
        other = lax.rem(sec + step, nsec)
        pl.semaphore_signal(
            barrier, inc=1, device_id=(tile, other), device_id_type=MESH
        )
        pl.semaphore_signal(
            barrier, inc=1, device_id=(chip * 2 + 1 - core, other), device_id_type=MESH
        )

    a = a_ref[...]
    a_high, a_low = split(a)
    a_both = jnp.concatenate([a_high, a_low], axis=1)

    def times_cable(x):
        high, low = split(x)
        return jnp.dot(
            a_both, jnp.concatenate([high, high], axis=0), preferred_element_type=F32
        ) + jnp.dot(a_high, low, preferred_element_type=F32)

    gt = g_ref[...].T
    row = lax.broadcasted_iota(jnp.int32, (seg, cells), 0)
    at_end = jnp.where((row == 0) | (row == seg - 1), 0.5, 0.0)
    keep = 1.0 - TIME_STEP * gt - at_end
    leak = gt * e_ref[...].T
    zs[0] = v_ref[...].T
    hl[0] = jnp.broadcast_to(a[:, 0:1] * 0.5, (seg, cells))
    hr[0] = jnp.broadcast_to(a[:, seg - 1 : seg] * 0.5, (seg, cells))

    for k in range(STEPS):
        driven = d_ref[k].astype(F32).T
        rhs = keep * zs[k] + TIME_STEP * (leak + driven)
        if k < STEPS - 1:
            after = times_cable(
                jnp.concatenate([rhs, keep * hl[k], keep * hr[k]], axis=1)
            )
            zs[k + 1] = after[:, :cells]
            hl[k + 1] = after[:, cells : 2 * cells]
            hr[k + 1] = after[:, 2 * cells :]
        else:
            zs[k + 1] = times_cable(rhs)

    for k in range(LAGS):
        ends[pl.ds(k, 1), :] = zs[k, pl.ds(0, 1), :]
        ends[pl.ds(8 + k, 1), :] = zs[k, pl.ds(seg - 1, 1), :]
        ends[pl.ds(16 + k, 1), :] = hl[k, pl.ds(0, 1), :]
        ends[pl.ds(24 + k, 1), :] = hl[k, pl.ds(seg - 1, 1), :]
        ends[pl.ds(32 + k, 1), :] = hr[k, pl.ds(0, 1), :]
        ends[pl.ds(40 + k, 1), :] = hr[k, pl.ds(seg - 1, 1), :]

    own = jnp.broadcast_to(own_ref[...].astype(F32), (cells, cells))
    before = lax.broadcasted_iota(jnp.int32, (cells, cells), 0) < (
        lax.broadcasted_iota(jnp.int32, (cells, cells), 1)
    )
    same = jnp.where(before & (own == own.T), 1.0, 0.0)
    rank = jnp.sum(same, axis=0, keepdims=True)
    placed = own_ref[...] * CAP + rank.astype(jnp.int32)
    blocks = 8
    out_rows = ntile * ROWS
    target = jnp.concatenate([placed * HALF + k for k in range(HALF)], axis=1)

    def build_pick(b, carry):
        size = out_rows // blocks
        base = pl.multiple_of(b * size, size)
        rows = base + lax.broadcasted_iota(jnp.int32, (size, HALF * cells), 0)
        pick[pl.ds(base, size), :] = jnp.where(rows == target, 1.0, 0.0).astype(BF16)
        return carry

    lax.fori_loop(0, blocks, build_pick, 0)

    count = jnp.broadcast_to(cnt_ref[...].astype(F32), (8, ntile)).astype(BF16)
    source = lax.broadcasted_iota(jnp.int32, (ntile, out_rows), 0)
    lane = lax.broadcasted_iota(jnp.int32, (ntile, out_rows), 1)
    lane_source = lax.div(lane, ROWS)
    own_count = jnp.where(source == lane_source, 1.0, 0.0).astype(BF16)
    earlier = jnp.where(source < lane_source, 1.0, 0.0).astype(BF16)
    lane_count = jnp.dot(count, own_count, preferred_element_type=F32)[0:1]
    lane_start = jnp.dot(count, earlier, preferred_element_type=F32)[0:1]
    lane_row = lax.broadcasted_iota(jnp.int32, (1, out_rows), 1)
    lane_rank = lax.rem(lax.div(lane_row, HALF), CAP)
    lane_step = lax.rem(lane_row, HALF)
    slot_row = jnp.where(
        lane_rank < lane_count.astype(jnp.int32),
        (lane_start.astype(jnp.int32) + lane_rank) * HALF + lane_step,
        -1,
    )

    def build_place(b, carry):
        size = cells * HALF // blocks
        base = pl.multiple_of(b * size, size)
        rows = base + lax.broadcasted_iota(jnp.int32, (size, out_rows), 0)
        place[pl.ds(base, size), :] = jnp.where(rows == slot_row, 1.0, 0.0).astype(BF16)
        return carry

    lax.fori_loop(0, blocks, build_place, 0)

    contact = lax.broadcasted_iota(jnp.int32, (chips, cells), 0)
    choose = []
    for t in range(2):
        wide = jnp.broadcast_to(pat_ref[:, t : t + 1].astype(F32), (cells, cells)).T
        choose.append(
            jnp.where(wide[:chips].astype(jnp.int32) == contact, 1.0, 0.0).astype(BF16)
        )
    choose = jnp.concatenate(choose + choose, axis=1)

    pl.semaphore_wait(barrier, ntile - 1 + 2 * (nsec - 1))

    for step in range(1, nsec):
        pltpu.make_async_remote_copy(
            src_ref=ends,
            dst_ref=got.at[sec],
            send_sem=send_sem.at[0],
            recv_sem=recv_sem.at[0],
            device_id=(tile, lax.rem(sec + step, nsec)),
            device_id_type=MESH,
        ).start()
    pltpu.make_async_copy(ends, got.at[sec], recv_sem.at[0]).start()
    hpad[:, :, 0:8, :] = jnp.zeros((nsec, 4, 8, cells), F32)
    pltpu.make_async_copy(got, got, recv_sem.at[0]).wait()

    first_of = [got[s, 0:8, :] for s in range(nsec)]
    last_of = [got[s, 8:16, :] for s in range(nsec)]
    for s in range(nsec):
        for q in range(4):
            hpad[s, q, 8:16, :] = got[s, 16 + 8 * q : 24 + 8 * q, :]
    for j in range(STEPS - 1):
        lasts = [jnp.broadcast_to(x[j : j + 1], (8, cells)) for x in last_of]
        firsts = [jnp.broadcast_to(x[j : j + 1], (8, cells)) for x in first_of]
        for s in range(nsec):
            for q, side in ((0, s - 1), (2, s + 1)):
                if 0 <= side < nsec:
                    end = lasts[side] if q == 0 else firsts[side]
                    first_of[s] += hpad[s, q, pl.ds(7 - j, 8), :] * end
                    last_of[s] += hpad[s, q + 1, pl.ds(7 - j, 8), :] * end
    left = jnp.zeros((8, cells), F32)
    right = jnp.zeros((8, cells), F32)
    for s in range(nsec):
        if s > 0:
            left = jnp.where(sec == s, last_of[s - 1], left)
        if s < nsec - 1:
            right = jnp.where(sec == s, first_of[s + 1], right)

    g = g_ref[...]
    e = e_ref[...]
    for k in range(1, STEPS + 1):
        total = zs[k]
        for j in range(k):
            total += hl[k - 1 - j] * left[j : j + 1] + hr[k - 1 - j] * right[j : j + 1]
        now = total.T
        current = (g * (now - e) - d_ref[k - 1].astype(F32)).astype(BF16)
        c, k_in = divmod(k - 1, HALF)
        cur[c, k_in * cells : (k_in + 1) * cells, :] = current
        if k == STEPS:
            fv_ref[...] = now
        if k_in == HALF - 1:
            packed = jnp.dot(pick[...], cur[c], preferred_element_type=F32)
            outs[c] = packed.astype(BF16).reshape(ntile, ROWS, seg)

            def send(o, carry, c=c):
                peer = tile_peer(o)
                pltpu.make_async_remote_copy(
                    src_ref=outs.at[c, peer],
                    dst_ref=recv.at[c, tile],
                    send_sem=send_sem.at[1 + c],
                    recv_sem=recv_sem.at[1 + c],
                    device_id=(peer, sec),
                    device_id_type=MESH,
                ).start()
                return carry

            lax.fori_loop(0, ntile - 1, send, 0)
            pltpu.make_async_copy(
                outs.at[c, tile], recv.at[c, tile], recv_sem.at[1 + c]
            ).start()

    group = ROWS // HALF
    row16 = lax.broadcasted_iota(jnp.int32, (ROWS, seg), 0)
    masks = [
        jnp.where(lax.div(row16, HALF) == n, 1.0, 0.0).astype(BF16)
        for n in range(group)
    ]
    w_copy.wait()
    for c in range(2):
        pltpu.make_async_copy(recv.at[c], recv.at[c], recv_sem.at[1 + c]).wait()
        ordered[...] = (
            jnp.dot(
                place[...],
                recv[c].reshape(out_rows, seg),
                preferred_element_type=F32,
            )
            .astype(BF16)
            .reshape(cells // group, ROWS, seg)
        )

        def read(n, carry, c=c):
            x = ordered[n]
            left_side = jnp.concatenate([x * mask for mask in masks], axis=1)
            for t in range(2):
                right_side = w_ref[pl.ds(n * group, group), t].reshape(group * seg, -1)
                tiles[c, t, pl.ds(pl.multiple_of(n * ROWS, ROWS), ROWS), :] = jnp.dot(
                    left_side, right_side, preferred_element_type=F32
                )
            return carry

        lax.fori_loop(0, cells // group, read, 0, unroll=4)

        for k_in in range(HALF):
            sums = jnp.concatenate(
                [tiles[c, t, pl.ds(k_in, cells, stride=HALF), :] for t in range(2)],
                axis=0,
            )
            high, low = split(sums)
            part[pl.ds(c * HALF + k_in, chips, stride=STEPS), :] = jnp.dot(
                choose,
                jnp.concatenate([high, low], axis=0),
                preferred_element_type=F32,
            )

    def give(o, carry):
        peer = chip_peer(o)
        pltpu.make_async_remote_copy(
            src_ref=part.at[pl.ds(pl.multiple_of(peer * STEPS, STEPS), STEPS)],
            dst_ref=first.at[chip],
            send_sem=send_sem.at[3],
            recv_sem=recv_sem.at[3],
            device_id=(peer * 2 + core, sec),
            device_id_type=MESH,
        ).start()
        return carry

    lax.fori_loop(0, chips - 1, give, 0)
    pltpu.make_async_copy(
        part.at[pl.ds(pl.multiple_of(chip * STEPS, STEPS), STEPS)],
        first.at[chip],
        recv_sem.at[3],
    ).start()
    pltpu.make_async_copy(first, first, recv_sem.at[3]).wait()
    mine[...] = jnp.sum(first[...], axis=0)

    for step in range(nsec):
        for flip in range(2):
            if step or flip:
                other_sec = lax.rem(sec + step, nsec)
                other_core = lax.rem(core + flip, 2)
                pltpu.make_async_remote_copy(
                    src_ref=mine,
                    dst_ref=second.at[line],
                    send_sem=send_sem.at[4],
                    recv_sem=recv_sem.at[4],
                    device_id=(chip * 2 + other_core, other_sec),
                    device_id_type=MESH,
                ).start()
    pltpu.make_async_copy(mine, second.at[line], recv_sem.at[4]).start()
    pltpu.make_async_copy(second, second, recv_sem.at[4]).wait()
    width = probe_ref.shape[1]
    summed = jnp.sum(second[...], axis=0)
    probe_ref[...] = pltpu.roll(summed, lax.rem(seg - line * width, seg), 1)[:, :width]

    pltpu.make_async_copy(got.at[pl.ds(0, nsec - 1)], got.at[pl.ds(0, nsec - 1)], send_sem.at[0]).wait()
    for c in range(2):
        sent = outs.at[c, pl.ds(0, ntile - 1)]
        pltpu.make_async_copy(sent, sent, send_sem.at[1 + c]).wait()
    given = first.at[pl.ds(0, chips - 1)]
    pltpu.make_async_copy(given, given, send_sem.at[3]).wait()
    shared = second.at[pl.ds(0, 2 * nsec - 1)]
    pltpu.make_async_copy(shared, shared, send_sem.at[4]).wait()


def on_device(ny, nz, nsec, width, voltage, conductance, reversal, drive, inv_cable, owner_map, peer_counts, pattern, transfer):
    cells, seg = voltage.shape
    chips = ny * nz
    ntile = 2 * chips
    vmem = pl.BlockSpec(memory_space=pltpu.VMEM)
    rows = ntile * ROWS
    return pl.pallas_call(
        functools.partial(kernel, ny, nz, nsec),
        out_shape=(
            jax.ShapeDtypeStruct((cells, seg), F32),
            jax.ShapeDtypeStruct((STEPS, width), F32),
        ),
        in_specs=[vmem] * 8 + [pl.BlockSpec(memory_space=pl.ANY)],
        out_specs=(vmem, vmem),
        scratch_shapes=[
            pltpu.VMEM(transfer.shape[1:], BF16),
            pltpu.VMEM((STEPS + 1, seg, cells), F32),
            pltpu.VMEM((LAGS, seg, cells), F32),
            pltpu.VMEM((LAGS, seg, cells), F32),
            pltpu.VMEM((48, cells), F32),
            pltpu.VMEM((nsec, 48, cells), F32),
            pltpu.VMEM((nsec, 4, 16, cells), F32),
            pltpu.VMEM((rows, HALF * cells), BF16),
            pltpu.VMEM((cells * HALF, rows), BF16),
            pltpu.VMEM((2, HALF * cells, seg), BF16),
            pltpu.VMEM((2, ntile, ROWS, seg), BF16),
            pltpu.VMEM((2, ntile, ROWS, seg), BF16),
            pltpu.VMEM((cells // 4, ROWS, seg), BF16),
            pltpu.VMEM((2, 2, cells * HALF, seg), F32),
            pltpu.VMEM((chips * STEPS, seg), F32),
            pltpu.VMEM((chips, STEPS, seg), F32),
            pltpu.VMEM((STEPS, seg), F32),
            pltpu.VMEM((2 * nsec, STEPS, seg), F32),
            pltpu.SemaphoreType.DMA,
            pltpu.SemaphoreType.DMA((5,)),
            pltpu.SemaphoreType.DMA((5,)),
        ],
        compiler_params=pltpu.CompilerParams(
            collective_id=0, has_side_effects=True, vmem_limit_bytes=60 * 1024 * 1024
        ),
        name="cable_probe",
    )(
        voltage,
        conductance,
        reversal,
        drive,
        inv_cable,
        owner_map.reshape(1, -1),
        peer_counts,
        pattern[0],
        transfer,
    )


def solution(mesh):
    ntile, nsec = mesh.shape["tile"], mesh.shape["sec"]
    chips = ntile // 2
    nz = 8 if chips % 8 == 0 else 2
    ny = chips // nz
    width = chips * 128 // (ntile * nsec)
    placed = (
        P("tile", "sec"),
        P("tile", "sec"),
        P("tile", "sec"),
        P(None, "tile", "sec"),
        P(),
        P("tile"),
        P("tile", None),
        P("sec", "tile", None),
        P("sec", "tile", None, None, None),
    )
    return jax.shard_map(
        functools.partial(on_device, ny, nz, nsec, width),
        mesh=mesh,
        in_specs=placed,
        out_specs=(P("tile", "sec"), P(None, ("tile", "sec"))),
        check_vma=False,
    )
```

```python
import functools

import jax
import jax.numpy as jnp
from jax import lax
from jax.experimental import pallas as pl
from jax.experimental.pallas import tpu as pltpu
from jax.sharding import PartitionSpec as P

MESH = pl.DeviceIdType.MESH
F32 = jnp.float32
BF16 = jnp.bfloat16

STEPS = 8
HALF = 4
CAP = 4
ROWS = CAP * HALF
LAGS = 8
TIME_STEP = 0.25


def far_first(index, count):
    half = lax.div(index + 1, 2)
    return count // 2 + half * (1 - 2 * lax.rem(index, 2))


def split(x):
    high = x.astype(BF16)
    return high, (x - high.astype(F32)).astype(BF16)


def kernel(
    ny,
    nz,
    nsec,
    v_hbm,
    g_hbm,
    e_hbm,
    d_hbm,
    a_hbm,
    own_hbm,
    cnt_hbm,
    pat_hbm,
    w_hbm,
    fv_ref,
    probe_ref,
    v_ref,
    g_ref,
    e_ref,
    d_ref,
    a_ref,
    own_ref,
    cnt_ref,
    pat_ref,
    w_ref,
    zs,
    hl,
    hr,
    ends,
    got,
    hpad,
    zpad,
    pick,
    place,
    cur,
    outs,
    recv,
    ordered,
    tiles,
    part,
    first,
    mine,
    second,
    in_sem,
    w_sem,
    round_sem,
    send_sem,
    recv_sem,
):
    chips = ny * nz
    ntile = 2 * chips
    cells, seg = v_ref.shape
    tile = lax.axis_index("tile")
    sec = lax.axis_index("sec")
    core = lax.rem(tile, 2)
    chip = lax.div(tile, 2)
    my_y = lax.div(chip, nz)
    my_z = lax.rem(chip, nz)
    line = core * nsec + sec

    def chip_at(dy, dz):
        return lax.rem(my_y + dy, ny) * nz + lax.rem(my_z + dz, nz)

    def tile_peer(o):
        pair = lax.rem(o, 2 * ny)
        dz = far_first(lax.div(o, 2 * ny), nz)
        dy = far_first(lax.div(pair, 2), ny)
        return chip_at(dy, dz) * 2 + lax.rem(core + 1 + lax.rem(pair, 2), 2)

    def chip_peer(o):
        return chip_at(far_first(lax.rem(o, ny), ny), far_first(lax.div(o, ny), nz))

    barrier = pltpu.get_barrier_semaphore()

    def signal(sem, peer, peer_sec):
        pl.semaphore_signal(
            sem, inc=1, device_id=(peer, peer_sec), device_id_type=MESH
        )

    for step in range(1, nsec):
        signal(barrier, tile, lax.rem(sec + step, nsec))
    for dz in (2, nz - 2, 1, nz - 1):
        signal(barrier, chip_at(0, dz) * 2 + core, sec)
    for dy in (2, 1, 3):
        signal(barrier, chip_at(dy, 0) * 2 + core, sec)
    signal(barrier, chip * 2 + 1 - core, sec)

    loads = []
    for n, (src, dst) in enumerate(
        (
            (a_hbm, a_ref),
            (g_hbm, g_ref),
            (e_hbm, e_ref),
            (v_hbm, v_ref),
            (d_hbm, d_ref),
            (own_hbm, own_ref),
            (cnt_hbm, cnt_ref),
            (pat_hbm, pat_ref),
        )
    ):
        loads.append(pltpu.make_async_copy(src, dst, in_sem.at[n]))
        loads[-1].start()
    w_copy = pltpu.make_async_copy(w_hbm.at[0], w_ref, w_sem)
    w_copy.start()
    for load in loads:
        load.wait()

    a = a_ref[...]
    a_high, a_low = split(a)
    a_both = jnp.concatenate([a_high, a_low], axis=1)

    def times_cable(x):
        high, low = split(x)
        return jnp.dot(
            a_both, jnp.concatenate([high, high], axis=0), preferred_element_type=F32
        ) + jnp.dot(a_high, low, preferred_element_type=F32)

    gt = g_ref[...].T
    row = lax.broadcasted_iota(jnp.int32, (seg, cells), 0)
    at_end = jnp.where((row == 0) | (row == seg - 1), 0.5, 0.0)
    keep = 1.0 - TIME_STEP * gt - at_end
    leak = gt * e_ref[...].T
    zs[0] = v_ref[...].T
    hl[0] = jnp.broadcast_to(a[:, 0:1] * 0.5, (seg, cells))
    hr[0] = jnp.broadcast_to(a[:, seg - 1 : seg] * 0.5, (seg, cells))

    def advance(k):
        driven = d_ref[k].astype(F32).T
        rhs = keep * zs[k] + TIME_STEP * (leak + driven)
        if k < STEPS - 1:
            after = times_cable(
                jnp.concatenate([rhs, keep * hl[k], keep * hr[k]], axis=1)
            )
            zs[k + 1] = after[:, :cells]
            hl[k + 1] = after[:, cells : 2 * cells]
            hr[k + 1] = after[:, 2 * cells :]
        else:
            zs[k + 1] = times_cable(rhs)

    def offer(c):
        for k in range(HALF):
            at = c * HALF + k
            for n, source in enumerate((zs, hl, hr)):
                ends[c, pl.ds(2 * HALF * n + k, 1), :] = source[at, pl.ds(0, 1), :]
                ends[c, pl.ds(2 * HALF * n + HALF + k, 1), :] = source[
                    at, pl.ds(seg - 1, 1), :
                ]
        for step in range(1, nsec):
            pltpu.make_async_remote_copy(
                src_ref=ends.at[c],
                dst_ref=got.at[c, sec],
                send_sem=send_sem.at[5 + c],
                recv_sem=recv_sem.at[5 + c],
                device_id=(tile, lax.rem(sec + step, nsec)),
                device_id_type=MESH,
            ).start()
        pltpu.make_async_copy(ends.at[c], got.at[c, sec], recv_sem.at[5 + c]).start()

    for k in range(HALF - 1):
        advance(k)
    pl.semaphore_wait(barrier, nsec - 1 + 8)
    offer(0)
    for dz in (2, nz - 2):
        signal(round_sem.at[0], chip_at(0, dz) * 2 + core, sec)
    for k in range(HALF - 1, STEPS - 1):
        advance(k)
    offer(1)
    advance(STEPS - 1)
    hpad[:, :, 0:8, :] = jnp.zeros((nsec, 4, 8, cells), F32)

    own = jnp.broadcast_to(own_ref[...].astype(F32), (cells, cells))
    before = lax.broadcasted_iota(jnp.int32, (cells, cells), 0) < (
        lax.broadcasted_iota(jnp.int32, (cells, cells), 1)
    )
    same = jnp.where(before & (own == own.T), 1.0, 0.0)
    rank = jnp.sum(same, axis=0, keepdims=True)
    placed = own_ref[...] * CAP + rank.astype(jnp.int32)
    blocks = 8
    out_rows = ntile * ROWS
    target = jnp.concatenate([placed * HALF + k for k in range(HALF)], axis=1)

    def build_pick(b, carry):
        size = out_rows // blocks
        base = pl.multiple_of(b * size, size)
        rows = base + lax.broadcasted_iota(jnp.int32, (size, HALF * cells), 0)
        pick[pl.ds(base, size), :] = jnp.where(rows == target, 1.0, 0.0).astype(BF16)
        return carry

    lax.fori_loop(0, blocks, build_pick, 0)

    def meet(c):
        pltpu.make_async_copy(got.at[c], got.at[c], recv_sem.at[5 + c]).wait()
        known = (c + 1) * HALF
        for s in range(nsec):
            for q in range(2):
                zpad[s, q, c * HALF : known, :] = got[c, s, q * HALF : (q + 1) * HALF, :]
            for q in range(4):
                hpad[s, q, 8 + c * HALF : 8 + known, :] = got[
                    c, s, (2 + q) * HALF : (3 + q) * HALF, :
                ]
        first_of = [zpad[s, 0, 0:known, :] for s in range(nsec)]
        last_of = [zpad[s, 1, 0:known, :] for s in range(nsec)]
        for j in range(known - 1):
            lasts = [jnp.broadcast_to(x[j : j + 1], (known, cells)) for x in last_of]
            firsts = [jnp.broadcast_to(x[j : j + 1], (known, cells)) for x in first_of]
            for s in range(nsec):
                for q, side in ((0, s - 1), (2, s + 1)):
                    if 0 <= side < nsec:
                        end = lasts[side] if q == 0 else firsts[side]
                        first_of[s] += hpad[s, q, pl.ds(7 - j, known), :] * end
                        last_of[s] += hpad[s, q + 1, pl.ds(7 - j, known), :] * end
        left = jnp.zeros((known, cells), F32)
        right = jnp.zeros((known, cells), F32)
        for s in range(nsec):
            if s > 0:
                left = jnp.where(sec == s, last_of[s - 1], left)
            if s < nsec - 1:
                right = jnp.where(sec == s, first_of[s + 1], right)
        return left, right

    def currents(c):
        left, right = meet(c)
        for k_in in range(HALF):
            k = c * HALF + k_in + 1
            total = zs[k]
            for j in range(k):
                total += (
                    hl[k - 1 - j] * left[j : j + 1] + hr[k - 1 - j] * right[j : j + 1]
                )
            now = total.T
            driven = d_ref[k - 1].astype(F32)
            current = (g_ref[...] * (now - e_ref[...]) - driven).astype(BF16)
            cur[c, k_in * cells : (k_in + 1) * cells, :] = current
            if k == STEPS:
                fv_ref[...] = now
        packed = jnp.dot(pick[...], cur[c], preferred_element_type=F32)
        outs[c] = packed.astype(BF16).reshape(ntile, ROWS, seg)

    def deliver(c):
        def send(o, carry):
            peer = tile_peer(o)
            pltpu.make_async_remote_copy(
                src_ref=outs.at[c, peer],
                dst_ref=recv.at[c, tile],
                send_sem=send_sem.at[1 + c],
                recv_sem=recv_sem.at[1 + c],
                device_id=(peer, sec),
                device_id_type=MESH,
            ).start()
            return carry

        lax.fori_loop(0, ntile - 1, send, 0)
        pltpu.make_async_copy(
            outs.at[c, tile], recv.at[c, tile], recv_sem.at[1 + c]
        ).start()

    pl.semaphore_wait(round_sem.at[0], 2)
    for dy in (2, 1, 3):
        signal(round_sem.at[1], chip_at(dy, 0) * 2 + core, sec)
    currents(0)
    pl.semaphore_wait(round_sem.at[1], 3)
    signal(round_sem.at[2], chip * 2 + 1 - core, sec)
    pl.semaphore_wait(round_sem.at[2], 1)
    deliver(0)
    currents(1)
    deliver(1)

    count = jnp.broadcast_to(cnt_ref[...].astype(F32), (8, ntile)).astype(BF16)
    source = lax.broadcasted_iota(jnp.int32, (ntile, out_rows), 0)
    lane = lax.broadcasted_iota(jnp.int32, (ntile, out_rows), 1)
    lane_source = lax.div(lane, ROWS)
    own_count = jnp.where(source == lane_source, 1.0, 0.0).astype(BF16)
    earlier = jnp.where(source < lane_source, 1.0, 0.0).astype(BF16)
    lane_count = jnp.dot(count, own_count, preferred_element_type=F32)[0:1]
    lane_start = jnp.dot(count, earlier, preferred_element_type=F32)[0:1]
    lane_row = lax.broadcasted_iota(jnp.int32, (1, out_rows), 1)
    lane_rank = lax.rem(lax.div(lane_row, HALF), CAP)
    lane_step = lax.rem(lane_row, HALF)
    slot_row = jnp.where(
        lane_rank < lane_count.astype(jnp.int32),
        (lane_start.astype(jnp.int32) + lane_rank) * HALF + lane_step,
        -1,
    )

    def build_place(b, carry):
        size = cells * HALF // blocks
        base = pl.multiple_of(b * size, size)
        rows = base + lax.broadcasted_iota(jnp.int32, (size, out_rows), 0)
        place[pl.ds(base, size), :] = jnp.where(rows == slot_row, 1.0, 0.0).astype(BF16)
        return carry

    lax.fori_loop(0, blocks, build_place, 0)

    contact = lax.broadcasted_iota(jnp.int32, (chips, cells), 0)
    choose = jnp.concatenate(
        [
            jnp.where(pat_ref[t : t + 1, :] == contact, 1.0, 0.0).astype(BF16)
            for t in (0, 1, 0, 1)
        ],
        axis=1,
    )

    group = ROWS // HALF
    row16 = lax.broadcasted_iota(jnp.int32, (ROWS, seg), 0)
    masks = [
        jnp.where(lax.div(row16, HALF) == n, 1.0, 0.0).astype(BF16)
        for n in range(group)
    ]
    w_copy.wait()
    for c in range(2):
        pltpu.make_async_copy(recv.at[c], recv.at[c], recv_sem.at[1 + c]).wait()
        ordered[...] = (
            jnp.dot(
                place[...],
                recv[c].reshape(out_rows, seg),
                preferred_element_type=F32,
            )
            .astype(BF16)
            .reshape(cells // group, ROWS, seg)
        )

        def read(n, carry, c=c):
            x = ordered[n]
            left_side = jnp.concatenate([x * mask for mask in masks], axis=1)
            for t in range(2):
                right_side = w_ref[pl.ds(n * group, group), t].reshape(group * seg, -1)
                tiles[c, t, pl.ds(pl.multiple_of(n * ROWS, ROWS), ROWS), :] = jnp.dot(
                    left_side, right_side, preferred_element_type=F32
                )
            return carry

        lax.fori_loop(0, cells // group, read, 0, unroll=4)

        for k_in in range(HALF):
            sums = jnp.concatenate(
                [tiles[c, t, pl.ds(k_in, cells, stride=HALF), :] for t in range(2)],
                axis=0,
            )
            high, low = split(sums)
            part[pl.ds(c * HALF + k_in, chips, stride=STEPS), :] = jnp.dot(
                choose,
                jnp.concatenate([high, low], axis=0),
                preferred_element_type=F32,
            )

    def give(o, carry):
        peer = chip_peer(o)
        pltpu.make_async_remote_copy(
            src_ref=part.at[pl.ds(pl.multiple_of(peer * STEPS, STEPS), STEPS)],
            dst_ref=first.at[chip],
            send_sem=send_sem.at[3],
            recv_sem=recv_sem.at[3],
            device_id=(peer * 2 + core, sec),
            device_id_type=MESH,
        ).start()
        return carry

    lax.fori_loop(0, chips - 1, give, 0)
    pltpu.make_async_copy(
        part.at[pl.ds(pl.multiple_of(chip * STEPS, STEPS), STEPS)],
        first.at[chip],
        recv_sem.at[3],
    ).start()
    pltpu.make_async_copy(first, first, recv_sem.at[3]).wait()
    mine[...] = jnp.sum(first[...], axis=0)

    for step in range(nsec):
        for flip in range(2):
            if step or flip:
                other_sec = lax.rem(sec + step, nsec)
                other_core = lax.rem(core + flip, 2)
                pltpu.make_async_remote_copy(
                    src_ref=mine,
                    dst_ref=second.at[line],
                    send_sem=send_sem.at[4],
                    recv_sem=recv_sem.at[4],
                    device_id=(chip * 2 + other_core, other_sec),
                    device_id_type=MESH,
                ).start()
    pltpu.make_async_copy(mine, second.at[line], recv_sem.at[4]).start()
    pltpu.make_async_copy(second, second, recv_sem.at[4]).wait()
    width = probe_ref.shape[1]
    summed = jnp.sum(second[...], axis=0)
    probe_ref[...] = pltpu.roll(summed, lax.rem(seg - line * width, seg), 1)[:, :width]

    for c in range(2):
        told = got.at[c, pl.ds(0, nsec - 1)]
        pltpu.make_async_copy(told, told, send_sem.at[5 + c]).wait()
        sent = outs.at[c, pl.ds(0, ntile - 1)]
        pltpu.make_async_copy(sent, sent, send_sem.at[1 + c]).wait()
    given = first.at[pl.ds(0, chips - 1)]
    pltpu.make_async_copy(given, given, send_sem.at[3]).wait()
    shared = second.at[pl.ds(0, 2 * nsec - 1)]
    pltpu.make_async_copy(shared, shared, send_sem.at[4]).wait()


def on_device(ny, nz, nsec, width, voltage, conductance, reversal, drive, inv_cable, owner_map, peer_counts, pattern, transfer):
    cells, seg = voltage.shape
    chips = ny * nz
    ntile = 2 * chips
    vmem = pl.BlockSpec(memory_space=pltpu.VMEM)
    rows = ntile * ROWS
    return pl.pallas_call(
        functools.partial(kernel, ny, nz, nsec),
        out_shape=(
            jax.ShapeDtypeStruct((cells, seg), F32),
            jax.ShapeDtypeStruct((STEPS, width), F32),
        ),
        in_specs=[pl.BlockSpec(memory_space=pl.ANY)] * 9,
        out_specs=(vmem, vmem),
        scratch_shapes=[
            pltpu.VMEM((cells, seg), F32),
            pltpu.VMEM((cells, seg), F32),
            pltpu.VMEM((cells, seg), F32),
            pltpu.VMEM((STEPS, cells, seg), BF16),
            pltpu.VMEM((seg, seg), F32),
            pltpu.VMEM((1, cells), jnp.int32),
            pltpu.VMEM((1, ntile), jnp.int32),
            pltpu.VMEM((2, cells), jnp.int32),
            pltpu.VMEM(transfer.shape[1:], BF16),
            pltpu.VMEM((STEPS + 1, seg, cells), F32),
            pltpu.VMEM((LAGS, seg, cells), F32),
            pltpu.VMEM((LAGS, seg, cells), F32),
            pltpu.VMEM((2, 6 * HALF, cells), F32),
            pltpu.VMEM((2, nsec, 6 * HALF, cells), F32),
            pltpu.VMEM((nsec, 4, 16, cells), F32),
            pltpu.VMEM((nsec, 2, 8, cells), F32),
            pltpu.VMEM((rows, HALF * cells), BF16),
            pltpu.VMEM((cells * HALF, rows), BF16),
            pltpu.VMEM((2, HALF * cells, seg), BF16),
            pltpu.VMEM((2, ntile, ROWS, seg), BF16),
            pltpu.VMEM((2, ntile, ROWS, seg), BF16),
            pltpu.VMEM((cells // 4, ROWS, seg), BF16),
            pltpu.VMEM((2, 2, cells * HALF, seg), F32),
            pltpu.VMEM((chips * STEPS, seg), F32),
            pltpu.VMEM((chips, STEPS, seg), F32),
            pltpu.VMEM((STEPS, seg), F32),
            pltpu.VMEM((2 * nsec, STEPS, seg), F32),
            pltpu.SemaphoreType.DMA((8,)),
            pltpu.SemaphoreType.DMA,
            pltpu.SemaphoreType.REGULAR((3,)),
            pltpu.SemaphoreType.DMA((7,)),
            pltpu.SemaphoreType.DMA((7,)),
        ],
        compiler_params=pltpu.CompilerParams(
            collective_id=0, has_side_effects=True, vmem_limit_bytes=60 * 1024 * 1024
        ),
        name="cable_probe",
    )(
        voltage,
        conductance,
        reversal,
        drive,
        inv_cable,
        owner_map.reshape(1, -1),
        peer_counts,
        pattern[0].T,
        transfer,
    )


def solution(mesh):
    ntile, nsec = mesh.shape["tile"], mesh.shape["sec"]
    chips = ntile // 2
    nz = 8 if chips % 8 == 0 else 2
    ny = chips // nz
    width = chips * 128 // (ntile * nsec)
    placed = (
        P("tile", "sec"),
        P("tile", "sec"),
        P("tile", "sec"),
        P(None, "tile", "sec"),
        P(),
        P("tile"),
        P("tile", None),
        P("sec", "tile", None),
        P("sec", "tile", None, None, None),
    )
    return jax.shard_map(
        functools.partial(on_device, ny, nz, nsec, width),
        mesh=mesh,
        in_specs=placed,
        out_specs=(P("tile", "sec"), P(None, ("tile", "sec"))),
        check_vma=False,
    )
```

```python
import functools

import jax
import jax.numpy as jnp
from jax import lax
from jax.experimental import pallas as pl
from jax.experimental.pallas import tpu as pltpu
from jax.sharding import PartitionSpec as P

MESH = pl.DeviceIdType.MESH
F32 = jnp.float32
BF16 = jnp.bfloat16

STEPS = 8
HALF = 4
CAP = 4
ROWS = CAP * HALF
LAGS = 8
TIME_STEP = 0.25


def far_first(index, count):
    half = lax.div(index + 1, 2)
    return count // 2 + half * (1 - 2 * lax.rem(index, 2))


def split(x):
    high = x.astype(BF16)
    return high, (x - high.astype(F32)).astype(BF16)


def kernel(
    ny,
    nz,
    nsec,
    v_hbm,
    g_hbm,
    e_hbm,
    d_hbm,
    a_hbm,
    own_hbm,
    cnt_hbm,
    pat_hbm,
    w_hbm,
    fv_ref,
    probe_ref,
    v_ref,
    g_ref,
    e_ref,
    d_ref,
    a_ref,
    own_ref,
    cnt_ref,
    pat_ref,
    w_ref,
    zs,
    hl,
    hr,
    ends,
    got,
    hpad,
    zpad,
    pick,
    place,
    cur,
    outs,
    recv,
    ordered,
    tiles,
    part,
    partial,
    first,
    mine,
    second,
    in_sem,
    w_sem,
    round_sem,
    send_sem,
    recv_sem,
):
    chips = ny * nz
    ntile = 2 * chips
    cells, seg = v_ref.shape
    tile = lax.axis_index("tile")
    sec = lax.axis_index("sec")
    core = lax.rem(tile, 2)
    chip = lax.div(tile, 2)
    my_y = lax.div(chip, nz)
    my_z = lax.rem(chip, nz)
    line = core * nsec + sec

    base_y = [lax.rem(my_y + dy, ny) * nz for dy in range(ny)]
    at_z = [lax.rem(my_z + dz, nz) for dz in range(nz)]
    y_order = (2, 1, 3)
    far = (4, 3, 5)
    near = (2, 6, 1, 7)

    def along_y(body):
        def step(index, carry):
            body(lax.rem(my_y + far_first(index, ny), ny) * nz)
            return carry

        lax.fori_loop(0, ny - 1, step, 0)

    barrier = pltpu.get_barrier_semaphore()

    def signal(sem, peer, peer_sec):
        pl.semaphore_signal(
            sem, inc=1, device_id=(peer, peer_sec), device_id_type=MESH
        )

    loads = []
    for n, (src, dst) in enumerate(
        (
            (a_hbm, a_ref),
            (g_hbm, g_ref),
            (e_hbm, e_ref),
            (v_hbm, v_ref),
            (d_hbm, d_ref),
            (own_hbm, own_ref),
            (cnt_hbm, cnt_ref),
            (pat_hbm, pat_ref),
        )
    ):
        loads.append(pltpu.make_async_copy(src, dst, in_sem.at[n]))
        loads[-1].start()
    for step in range(1, nsec):
        signal(barrier, tile, lax.rem(sec + step, nsec))
    for dz in (2, nz - 2, 1, nz - 1):
        signal(barrier, (base_y[0] + at_z[dz]) * 2 + core, sec)
    for dy in (2, 1, 3, 0):
        if dy:
            signal(barrier, (base_y[dy] + my_z) * 2 + core, sec)
        signal(barrier, (base_y[dy] + my_z) * 2 + 1 - core, sec)

    for load in loads[:5]:
        load.wait()
    w_copy = pltpu.make_async_copy(w_hbm.at[0], w_ref, w_sem)
    w_copy.start()

    a = a_ref[...]
    a_high, a_low = split(a)
    a_both = jnp.concatenate([a_high, a_low], axis=1)

    def times_cable(x):
        high, low = split(x)
        return jnp.dot(
            a_both, jnp.concatenate([high, high], axis=0), preferred_element_type=F32
        ) + jnp.dot(a_high, low, preferred_element_type=F32)

    gt = g_ref[...].T
    row = lax.broadcasted_iota(jnp.int32, (seg, cells), 0)
    at_end = jnp.where((row == 0) | (row == seg - 1), 0.5, 0.0)
    keep = 1.0 - TIME_STEP * gt - at_end
    leak = gt * e_ref[...].T
    zs[0] = v_ref[...].T
    hl[0] = jnp.broadcast_to(a[:, 0:1] * 0.5, (seg, cells))
    hr[0] = jnp.broadcast_to(a[:, seg - 1 : seg] * 0.5, (seg, cells))

    def advance(k):
        driven = d_ref[k].astype(F32).T
        rhs = keep * zs[k] + TIME_STEP * (leak + driven)
        if k < STEPS - 1:
            after = times_cable(
                jnp.concatenate([rhs, keep * hl[k], keep * hr[k]], axis=1)
            )
            zs[k + 1] = after[:, :cells]
            hl[k + 1] = after[:, cells : 2 * cells]
            hr[k + 1] = after[:, 2 * cells :]
        else:
            zs[k + 1] = times_cable(rhs)

    def offer(c):
        for k in range(HALF):
            at = c * HALF + k
            for n, source in enumerate((zs, hl, hr)):
                ends[c, pl.ds(2 * HALF * n + k, 1), :] = source[at, pl.ds(0, 1), :]
                ends[c, pl.ds(2 * HALF * n + HALF + k, 1), :] = source[
                    at, pl.ds(seg - 1, 1), :
                ]
        for step in range(1, nsec):
            pltpu.make_async_remote_copy(
                src_ref=ends.at[c],
                dst_ref=got.at[c, sec],
                send_sem=send_sem.at[5 + c],
                recv_sem=recv_sem.at[5 + c],
                device_id=(tile, lax.rem(sec + step, nsec)),
                device_id_type=MESH,
            ).start()
        pltpu.make_async_copy(ends.at[c], got.at[c, sec], recv_sem.at[5 + c]).start()

    for k in range(HALF - 1):
        advance(k)
    pl.semaphore_wait(barrier, nsec - 1 + 4 + 7)
    offer(0)
    for dy in (2, 1, 3, 0):
        if dy:
            signal(round_sem.at[0], (base_y[dy] + my_z) * 2 + core, sec)
        signal(round_sem.at[0], (base_y[dy] + my_z) * 2 + 1 - core, sec)
    for k in range(HALF - 1, STEPS - 1):
        advance(k)
    offer(1)
    advance(STEPS - 1)
    hpad[:, :, 0:8, :] = jnp.zeros((nsec, 4, 8, cells), F32)

    for load in loads[5:]:
        load.wait()

    own = jnp.broadcast_to(own_ref[...].astype(F32), (cells, cells))
    before = lax.broadcasted_iota(jnp.int32, (cells, cells), 0) < (
        lax.broadcasted_iota(jnp.int32, (cells, cells), 1)
    )
    same = jnp.where(before & (own == own.T), 1.0, 0.0)
    rank = jnp.sum(same, axis=0, keepdims=True)
    placed = own_ref[...] * CAP + rank.astype(jnp.int32)
    blocks = 8
    out_rows = ntile * ROWS
    target = jnp.concatenate([placed * HALF + k for k in range(HALF)], axis=1)

    def build_pick(b, carry):
        size = out_rows // blocks
        base = pl.multiple_of(b * size, size)
        rows = base + lax.broadcasted_iota(jnp.int32, (size, HALF * cells), 0)
        pick[pl.ds(base, size), :] = jnp.where(rows == target, 1.0, 0.0).astype(BF16)
        return carry

    lax.fori_loop(0, blocks, build_pick, 0)

    def meet(c):
        pltpu.make_async_copy(got.at[c], got.at[c], recv_sem.at[5 + c]).wait()
        known = (c + 1) * HALF
        for s in range(nsec):
            for q in range(2):
                zpad[s, q, c * HALF : known, :] = got[c, s, q * HALF : (q + 1) * HALF, :]
            for q in range(4):
                hpad[s, q, 8 + c * HALF : 8 + known, :] = got[
                    c, s, (2 + q) * HALF : (3 + q) * HALF, :
                ]
        first_of = [zpad[s, 0, 0:known, :] for s in range(nsec)]
        last_of = [zpad[s, 1, 0:known, :] for s in range(nsec)]
        for j in range(known - 1):
            lasts = [jnp.broadcast_to(x[j : j + 1], (known, cells)) for x in last_of]
            firsts = [jnp.broadcast_to(x[j : j + 1], (known, cells)) for x in first_of]
            for s in range(nsec):
                for q, side in ((0, s - 1), (2, s + 1)):
                    if 0 <= side < nsec:
                        end = lasts[side] if q == 0 else firsts[side]
                        first_of[s] += hpad[s, q, pl.ds(7 - j, known), :] * end
                        last_of[s] += hpad[s, q + 1, pl.ds(7 - j, known), :] * end
        left = jnp.zeros((known, cells), F32)
        right = jnp.zeros((known, cells), F32)
        for s in range(nsec):
            if s > 0:
                left = jnp.where(sec == s, last_of[s - 1], left)
            if s < nsec - 1:
                right = jnp.where(sec == s, first_of[s + 1], right)
        return left, right

    def currents(c):
        left, right = meet(c)
        for k_in in range(HALF):
            k = c * HALF + k_in + 1
            total = zs[k]
            for j in range(k):
                total += (
                    hl[k - 1 - j] * left[j : j + 1] + hr[k - 1 - j] * right[j : j + 1]
                )
            now = total.T
            driven = d_ref[k - 1].astype(F32)
            current = (g_ref[...] * (now - e_ref[...]) - driven).astype(BF16)
            cur[c, k_in * cells : (k_in + 1) * cells, :] = current
            if k == STEPS:
                fv_ref[...] = now
        packed = jnp.dot(pick[...], cur[c], preferred_element_type=F32)
        outs[c] = packed.astype(BF16).reshape(ntile, ROWS, seg)

    def deliver(c, offsets):
        def send(peer):
            pltpu.make_async_remote_copy(
                src_ref=outs.at[c, peer],
                dst_ref=recv.at[c, tile],
                send_sem=send_sem.at[1 + c],
                recv_sem=recv_sem.at[1 + c],
                device_id=(peer, sec),
                device_id_type=MESH,
            ).start()

        def send_all(base, at_own_z):
            for other in (1, 0):
                for dz in offsets:
                    at = (base + at_z[dz]) * 2
                    send(at + 1 - core if other else at + core)
            if at_own_z:
                send((base + my_z) * 2 + 1 - core)
                if at_own_z == 2:
                    send((base + my_z) * 2 + core)

        along_y(lambda base: send_all(base, 2 if offsets is near else 0))
        send_all(base_y[0], 1 if offsets is near else 0)
        if offsets is near:
            pltpu.make_async_copy(
                outs.at[c, tile], recv.at[c, tile], recv_sem.at[1 + c]
            ).start()

    currents(0)
    pl.semaphore_wait(round_sem.at[0], 7)
    for dz in (2, nz - 2):
        signal(round_sem.at[1], (base_y[0] + at_z[dz]) * 2 + core, sec)
    deliver(0, near)
    currents(1)
    pl.semaphore_wait(round_sem.at[1], 2)
    deliver(0, far)
    deliver(1, far)
    deliver(1, near)

    count = jnp.broadcast_to(cnt_ref[...].astype(F32), (8, ntile)).astype(BF16)
    source = lax.broadcasted_iota(jnp.int32, (ntile, out_rows), 0)
    lane = lax.broadcasted_iota(jnp.int32, (ntile, out_rows), 1)
    lane_source = lax.div(lane, ROWS)
    own_count = jnp.where(source == lane_source, 1.0, 0.0).astype(BF16)
    earlier = jnp.where(source < lane_source, 1.0, 0.0).astype(BF16)
    lane_count = jnp.dot(count, own_count, preferred_element_type=F32)[0:1]
    lane_start = jnp.dot(count, earlier, preferred_element_type=F32)[0:1]
    lane_row = lax.broadcasted_iota(jnp.int32, (1, out_rows), 1)
    lane_rank = lax.rem(lax.div(lane_row, HALF), CAP)
    lane_step = lax.rem(lane_row, HALF)
    slot_row = jnp.where(
        lane_rank < lane_count.astype(jnp.int32),
        (lane_start.astype(jnp.int32) + lane_rank) * HALF + lane_step,
        -1,
    )

    def build_place(b, carry):
        size = cells * HALF // blocks
        base = pl.multiple_of(b * size, size)
        rows = base + lax.broadcasted_iota(jnp.int32, (size, out_rows), 0)
        place[pl.ds(base, size), :] = jnp.where(rows == slot_row, 1.0, 0.0).astype(BF16)
        return carry

    lax.fori_loop(0, blocks, build_place, 0)

    contact = lax.broadcasted_iota(jnp.int32, (chips, cells), 0)
    choose = jnp.concatenate(
        [
            jnp.where(pat_ref[t : t + 1, :] == contact, 1.0, 0.0).astype(BF16)
            for t in (0, 1, 0, 1)
        ],
        axis=1,
    )

    group = ROWS // HALF
    row16 = lax.broadcasted_iota(jnp.int32, (ROWS, seg), 0)
    masks = [
        jnp.where(lax.div(row16, HALF) == n, 1.0, 0.0).astype(BF16)
        for n in range(group)
    ]
    w_copy.wait()
    for c in range(2):
        pltpu.make_async_copy(recv.at[c], recv.at[c], recv_sem.at[1 + c]).wait()
        ordered[...] = (
            jnp.dot(
                place[...],
                recv[c].reshape(out_rows, seg),
                preferred_element_type=F32,
            )
            .astype(BF16)
            .reshape(cells // group, ROWS, seg)
        )

        def read(n, carry, c=c):
            x = ordered[n]
            left_side = jnp.concatenate([x * mask for mask in masks], axis=1)
            right_side = jnp.concatenate(
                [
                    w_ref[pl.ds(n * group, group), t].reshape(group * seg, -1)
                    for t in range(2)
                ],
                axis=1,
            )
            both = jnp.dot(left_side, right_side, preferred_element_type=F32)
            for t in range(2):
                tiles[c, t, pl.ds(pl.multiple_of(n * ROWS, ROWS), ROWS), :] = both[
                    :, t * seg : (t + 1) * seg
                ]
            return carry

        lax.fori_loop(0, cells // group, read, 0, unroll=4)

        for k_in in range(HALF):
            sums = jnp.concatenate(
                [tiles[c, t, pl.ds(k_in, cells, stride=HALF), :] for t in range(2)],
                axis=0,
            )
            high, low = split(sums)
            part[pl.ds(c * HALF + k_in, chips, stride=STEPS), :] = jnp.dot(
                choose,
                jnp.concatenate([high, low], axis=0),
                preferred_element_type=F32,
            )

    partial[...] = part[...].astype(BF16).reshape(chips, STEPS, seg)

    def give(peer_chip):
        pltpu.make_async_remote_copy(
            src_ref=partial.at[peer_chip],
            dst_ref=first.at[chip],
            send_sem=send_sem.at[3],
            recv_sem=recv_sem.at[3],
            device_id=(peer_chip * 2 + core, sec),
            device_id_type=MESH,
        ).start()

    def give_all(base):
        for dz in far + near:
            give(base + at_z[dz])

    along_y(lambda base: (give_all(base), give(base + my_z)))
    give_all(base_y[0])
    pltpu.make_async_copy(partial.at[chip], first.at[chip], recv_sem.at[3]).start()
    pltpu.make_async_copy(first, first, recv_sem.at[3]).wait()
    mine[...] = jnp.sum(first[...].astype(F32), axis=0)

    for step in (2, 1, 3, 0):
        for flip in range(2):
            if step or flip:
                other_sec = lax.rem(sec + step, nsec)
                other_core = lax.rem(core + flip, 2)
                pltpu.make_async_remote_copy(
                    src_ref=mine,
                    dst_ref=second.at[line],
                    send_sem=send_sem.at[4],
                    recv_sem=recv_sem.at[4],
                    device_id=(chip * 2 + other_core, other_sec),
                    device_id_type=MESH,
                ).start()
    pltpu.make_async_copy(mine, second.at[line], recv_sem.at[4]).start()
    pltpu.make_async_copy(second, second, recv_sem.at[4]).wait()
    width = probe_ref.shape[1]
    summed = jnp.sum(second[...], axis=0)
    probe_ref[...] = pltpu.roll(summed, lax.rem(seg - line * width, seg), 1)[:, :width]

    for c in range(2):
        told = got.at[c, pl.ds(0, nsec - 1)]
        pltpu.make_async_copy(told, told, send_sem.at[5 + c]).wait()
        sent = outs.at[c, pl.ds(0, ntile - 1)]
        pltpu.make_async_copy(sent, sent, send_sem.at[1 + c]).wait()
    given = first.at[pl.ds(0, chips - 1)]
    pltpu.make_async_copy(given, given, send_sem.at[3]).wait()
    shared = second.at[pl.ds(0, 2 * nsec - 1)]
    pltpu.make_async_copy(shared, shared, send_sem.at[4]).wait()


def hand_over(fv_ref, probe_ref, fv_out, probe_out):
    fv_out[...] = fv_ref[...]
    probe_out[...] = probe_ref[...]


def on_device(ny, nz, nsec, width, voltage, conductance, reversal, drive, inv_cable, owner_map, peer_counts, pattern, transfer):
    cells, seg = voltage.shape
    chips = ny * nz
    ntile = 2 * chips
    vmem = pl.BlockSpec(memory_space=pltpu.VMEM)
    rows = ntile * ROWS
    results = pl.pallas_call(
        functools.partial(kernel, ny, nz, nsec),
        out_shape=(
            pltpu.VMEM((cells, seg), F32),
            pltpu.VMEM((STEPS, width), F32),
        ),
        in_specs=[pl.BlockSpec(memory_space=pl.ANY)] * 9,
        out_specs=(vmem, vmem),
        scratch_shapes=[
            pltpu.VMEM((cells, seg), F32),
            pltpu.VMEM((cells, seg), F32),
            pltpu.VMEM((cells, seg), F32),
            pltpu.VMEM((STEPS, cells, seg), BF16),
            pltpu.VMEM((seg, seg), F32),
            pltpu.VMEM((1, cells), jnp.int32),
            pltpu.VMEM((1, ntile), jnp.int32),
            pltpu.VMEM((2, cells), jnp.int32),
            pltpu.VMEM(transfer.shape[1:], BF16),
            pltpu.VMEM((STEPS + 1, seg, cells), F32),
            pltpu.VMEM((LAGS, seg, cells), F32),
            pltpu.VMEM((LAGS, seg, cells), F32),
            pltpu.VMEM((2, 6 * HALF, cells), F32),
            pltpu.VMEM((2, nsec, 6 * HALF, cells), F32),
            pltpu.VMEM((nsec, 4, 16, cells), F32),
            pltpu.VMEM((nsec, 2, 8, cells), F32),
            pltpu.VMEM((rows, HALF * cells), BF16),
            pltpu.VMEM((cells * HALF, rows), BF16),
            pltpu.VMEM((2, HALF * cells, seg), BF16),
            pltpu.VMEM((2, ntile, ROWS, seg), BF16),
            pltpu.VMEM((2, ntile, ROWS, seg), BF16),
            pltpu.VMEM((cells // 4, ROWS, seg), BF16),
            pltpu.VMEM((2, 2, cells * HALF, seg), F32),
            pltpu.VMEM((chips * STEPS, seg), F32),
            pltpu.VMEM((chips, STEPS, seg), BF16),
            pltpu.VMEM((chips, STEPS, seg), BF16),
            pltpu.VMEM((STEPS, seg), F32),
            pltpu.VMEM((2 * nsec, STEPS, seg), F32),
            pltpu.SemaphoreType.DMA((8,)),
            pltpu.SemaphoreType.DMA,
            pltpu.SemaphoreType.REGULAR((2,)),
            pltpu.SemaphoreType.DMA((7,)),
            pltpu.SemaphoreType.DMA((7,)),
        ],
        compiler_params=pltpu.CompilerParams(
            collective_id=0, has_side_effects=True, vmem_limit_bytes=60 * 1024 * 1024
        ),
        name="cable_probe",
    )(
        voltage,
        conductance,
        reversal,
        drive,
        inv_cable,
        owner_map.reshape(1, -1),
        peer_counts,
        pattern[0].T,
        transfer,
    )
    return pl.pallas_call(
        hand_over,
        out_shape=(
            jax.ShapeDtypeStruct((cells, seg), F32),
            jax.ShapeDtypeStruct((STEPS, width), F32),
        ),
        in_specs=[vmem, vmem],
        out_specs=(vmem, vmem),
        name="hand_over",
    )(*(pltpu.with_memory_space_constraint(x, pltpu.VMEM) for x in results))


def solution(mesh):
    ntile, nsec = mesh.shape["tile"], mesh.shape["sec"]
    chips = ntile // 2
    nz = 8 if chips % 8 == 0 else 2
    ny = chips // nz
    width = chips * 128 // (ntile * nsec)
    placed = (
        P("tile", "sec"),
        P("tile", "sec"),
        P("tile", "sec"),
        P(None, "tile", "sec"),
        P(),
        P("tile"),
        P("tile", None),
        P("sec", "tile", None),
        P("sec", "tile", None, None, None),
    )
    return jax.shard_map(
        functools.partial(on_device, ny, nz, nsec, width),
        mesh=mesh,
        in_specs=placed,
        out_specs=(P("tile", "sec"), P(None, ("tile", "sec"))),
        check_vma=False,
    )
```

```python
import functools

import jax
import jax.numpy as jnp
from jax import lax
from jax.experimental import pallas as pl
from jax.experimental.pallas import tpu as pltpu
from jax.sharding import PartitionSpec as P

MESH = pl.DeviceIdType.MESH
F32 = jnp.float32
BF16 = jnp.bfloat16

STEPS = 8
HALF = 4
CAP = 4
ROWS = CAP * HALF
LAGS = 8
TIME_STEP = 0.25


def far_first(index, count):
    half = lax.div(index + 1, 2)
    return count // 2 + half * (1 - 2 * lax.rem(index, 2))


def split(x):
    high = x.astype(BF16)
    return high, (x - high.astype(F32)).astype(BF16)


def kernel(
    ny,
    nz,
    nsec,
    v_hbm,
    g_hbm,
    e_hbm,
    d_hbm,
    a_hbm,
    own_hbm,
    cnt_hbm,
    pat_hbm,
    w_hbm,
    fv_ref,
    probe_ref,
    v_ref,
    g_ref,
    e_ref,
    d_ref,
    a_ref,
    own_ref,
    cnt_ref,
    pat_ref,
    w_ref,
    zs,
    hl,
    hr,
    ends,
    ends_out,
    ends_in,
    got,
    hpad,
    zpad,
    pick,
    place,
    cur,
    outs,
    recv,
    ordered,
    tiles,
    part,
    partial,
    first,
    mine,
    second,
    in_sem,
    w_sem,
    round_sem,
    send_sem,
    recv_sem,
):
    chips = ny * nz
    ntile = 2 * chips
    cells, seg = v_ref.shape
    tile = lax.axis_index("tile")
    sec = lax.axis_index("sec")
    core = lax.rem(tile, 2)
    chip = lax.div(tile, 2)
    my_y = lax.div(chip, nz)
    my_z = lax.rem(chip, nz)
    line = core * nsec + sec

    base_y = [lax.rem(my_y + dy, ny) * nz for dy in range(ny)]
    at_z = [lax.rem(my_z + dz, nz) for dz in range(nz)]
    y_order = (2, 1, 3)
    far = (4, 3, 5)
    near = (2, 6, 1, 7)

    def along_y(body):
        def step(index, carry):
            body(lax.rem(my_y + far_first(index, ny), ny) * nz)
            return carry

        lax.fori_loop(0, ny - 1, step, 0)

    barrier = pltpu.get_barrier_semaphore()

    def signal(sem, peer, peer_sec):
        pl.semaphore_signal(
            sem, inc=1, device_id=(peer, peer_sec), device_id_type=MESH
        )

    loads = []
    for n, (src, dst) in enumerate(
        (
            (a_hbm, a_ref),
            (g_hbm, g_ref),
            (e_hbm, e_ref),
            (v_hbm, v_ref),
            (d_hbm, d_ref),
            (own_hbm, own_ref),
            (cnt_hbm, cnt_ref),
            (pat_hbm, pat_ref),
        )
    ):
        loads.append(pltpu.make_async_copy(src, dst, in_sem.at[n]))
        loads[-1].start()
    for step in range(1, nsec):
        signal(barrier, tile, lax.rem(sec + step, nsec))
    for dz in (2, nz - 2, 1, nz - 1):
        signal(barrier, (base_y[0] + at_z[dz]) * 2 + core, sec)
    for dy in (2, 1, 3, 0):
        if dy:
            signal(barrier, (base_y[dy] + my_z) * 2 + core, sec)
        signal(barrier, (base_y[dy] + my_z) * 2 + 1 - core, sec)

    for load in loads[:5]:
        load.wait()
    w_copy = pltpu.make_async_copy(w_hbm.at[0], w_ref, w_sem)
    w_copy.start()

    a = a_ref[...]
    a_high, a_low = split(a)
    a_both = jnp.concatenate([a_high, a_low], axis=1)

    def times_cable(x):
        high, low = split(x)
        return jnp.dot(
            a_both, jnp.concatenate([high, high], axis=0), preferred_element_type=F32
        ) + jnp.dot(a_high, low, preferred_element_type=F32)

    gt = g_ref[...].T
    row = lax.broadcasted_iota(jnp.int32, (seg, cells), 0)
    at_end = jnp.where((row == 0) | (row == seg - 1), 0.5, 0.0)
    keep = 1.0 - TIME_STEP * gt - at_end
    leak = gt * e_ref[...].T
    zs[0] = v_ref[...].T
    hl[0] = jnp.broadcast_to(a[:, 0:1] * 0.5, (seg, cells))
    hr[0] = jnp.broadcast_to(a[:, seg - 1 : seg] * 0.5, (seg, cells))

    def advance(k):
        driven = d_ref[k].astype(F32).T
        rhs = keep * zs[k] + TIME_STEP * (leak + driven)
        if k < STEPS - 1:
            after = times_cable(
                jnp.concatenate([rhs, keep * hl[k], keep * hr[k]], axis=1)
            )
            zs[k + 1] = after[:, :cells]
            hl[k + 1] = after[:, cells : 2 * cells]
            hr[k + 1] = after[:, 2 * cells :]
        else:
            zs[k + 1] = times_cable(rhs)

    def offer(c):
        for k in range(HALF):
            at = c * HALF + k
            for n, source in enumerate((zs, hl, hr)):
                ends[c, pl.ds(2 * HALF * n + k, 1), :] = source[at, pl.ds(0, 1), :]
                ends[c, pl.ds(2 * HALF * n + HALF + k, 1), :] = source[
                    at, pl.ds(seg - 1, 1), :
                ]
        ends_out[c] = ends[c].astype(BF16)
        for step in (2, 1, 3):
            pltpu.make_async_remote_copy(
                src_ref=ends_out.at[c],
                dst_ref=ends_in.at[c, sec],
                send_sem=send_sem.at[5 + c],
                recv_sem=recv_sem.at[5 + c],
                device_id=(tile, lax.rem(sec + step, nsec)),
                device_id_type=MESH,
            ).start()
        pltpu.make_async_copy(
            ends_out.at[c], ends_in.at[c, sec], recv_sem.at[5 + c]
        ).start()

    for k in range(HALF - 1):
        advance(k)
    pl.semaphore_wait(barrier, nsec - 1 + 4 + 7)
    offer(0)
    for dy in (2, 1, 3, 0):
        if dy:
            signal(round_sem.at[0], (base_y[dy] + my_z) * 2 + core, sec)
        signal(round_sem.at[0], (base_y[dy] + my_z) * 2 + 1 - core, sec)
    for k in range(HALF - 1, STEPS - 1):
        advance(k)
    offer(1)
    advance(STEPS - 1)
    hpad[:, :, 0:8, :] = jnp.zeros((nsec, 4, 8, cells), F32)

    for load in loads[5:]:
        load.wait()

    own = jnp.broadcast_to(own_ref[...].astype(F32), (cells, cells))
    before = lax.broadcasted_iota(jnp.int32, (cells, cells), 0) < (
        lax.broadcasted_iota(jnp.int32, (cells, cells), 1)
    )
    same = jnp.where(before & (own == own.T), 1.0, 0.0)
    rank = jnp.sum(same, axis=0, keepdims=True)
    placed = own_ref[...] * CAP + rank.astype(jnp.int32)
    blocks = 8
    out_rows = ntile * ROWS
    target = jnp.concatenate([placed * HALF + k for k in range(HALF)], axis=1)

    def build_pick(b, carry):
        size = out_rows // blocks
        base = pl.multiple_of(b * size, size)
        rows = base + lax.broadcasted_iota(jnp.int32, (size, HALF * cells), 0)
        pick[pl.ds(base, size), :] = jnp.where(rows == target, 1.0, 0.0).astype(BF16)
        return carry

    lax.fori_loop(0, blocks, build_pick, 0)

    def meet(c):
        pltpu.make_async_copy(ends_in.at[c], ends_in.at[c], recv_sem.at[5 + c]).wait()
        got[c] = ends_in[c].astype(F32)
        known = (c + 1) * HALF
        for s in range(nsec):
            for q in range(2):
                zpad[s, q, c * HALF : known, :] = got[c, s, q * HALF : (q + 1) * HALF, :]
            for q in range(4):
                hpad[s, q, 8 + c * HALF : 8 + known, :] = got[
                    c, s, (2 + q) * HALF : (3 + q) * HALF, :
                ]
        first_of = [zpad[s, 0, 0:known, :] for s in range(nsec)]
        last_of = [zpad[s, 1, 0:known, :] for s in range(nsec)]
        for j in range(known - 1):
            lasts = [jnp.broadcast_to(x[j : j + 1], (known, cells)) for x in last_of]
            firsts = [jnp.broadcast_to(x[j : j + 1], (known, cells)) for x in first_of]
            for s in range(nsec):
                for q, side in ((0, s - 1), (2, s + 1)):
                    if 0 <= side < nsec:
                        end = lasts[side] if q == 0 else firsts[side]
                        first_of[s] += hpad[s, q, pl.ds(7 - j, known), :] * end
                        last_of[s] += hpad[s, q + 1, pl.ds(7 - j, known), :] * end
        left = jnp.zeros((known, cells), F32)
        right = jnp.zeros((known, cells), F32)
        for s in range(nsec):
            if s > 0:
                left = jnp.where(sec == s, last_of[s - 1], left)
            if s < nsec - 1:
                right = jnp.where(sec == s, first_of[s + 1], right)
        return left, right

    def currents(c):
        left, right = meet(c)
        for k_in in range(HALF):
            k = c * HALF + k_in + 1
            total = zs[k]
            for j in range(k):
                total += (
                    hl[k - 1 - j] * left[j : j + 1] + hr[k - 1 - j] * right[j : j + 1]
                )
            now = total.T
            driven = d_ref[k - 1].astype(F32)
            current = (g_ref[...] * (now - e_ref[...]) - driven).astype(BF16)
            cur[c, k_in * cells : (k_in + 1) * cells, :] = current
            if k == STEPS:
                fv_ref[...] = now

    def pack(c, base):
        size = 2 * nz * ROWS
        rows = pl.ds(pl.multiple_of(base * (2 * ROWS), size), size)
        packed = jnp.dot(pick[rows, :], cur[c], preferred_element_type=F32)
        outs[c, pl.ds(base * 2, 2 * nz)] = packed.astype(BF16).reshape(
            2 * nz, ROWS, seg
        )

    def deliver(c, offsets, fresh):
        def send(peer):
            pltpu.make_async_remote_copy(
                src_ref=outs.at[c, peer],
                dst_ref=recv.at[c, tile],
                send_sem=send_sem.at[1 + c],
                recv_sem=recv_sem.at[1 + c],
                device_id=(peer, sec),
                device_id_type=MESH,
            ).start()

        def send_all(base, at_own_z):
            if fresh:
                pack(c, base)
            for other in (1, 0):
                for dz in offsets:
                    at = (base + at_z[dz]) * 2
                    send(at + 1 - core if other else at + core)
            if at_own_z:
                send((base + my_z) * 2 + 1 - core)
                if at_own_z == 2:
                    send((base + my_z) * 2 + core)

        along_y(lambda base: send_all(base, 2 if offsets is near else 0))
        send_all(base_y[0], 1 if offsets is near else 0)
        if offsets is near:
            pltpu.make_async_copy(
                outs.at[c, tile], recv.at[c, tile], recv_sem.at[1 + c]
            ).start()

    currents(0)
    pl.semaphore_wait(round_sem.at[0], 7)
    for dz in (2, nz - 2):
        signal(round_sem.at[1], (base_y[0] + at_z[dz]) * 2 + core, sec)
    deliver(0, near, True)
    currents(1)
    pl.semaphore_wait(round_sem.at[1], 2)
    deliver(0, far, False)
    deliver(1, far, True)
    deliver(1, near, False)

    count = jnp.broadcast_to(cnt_ref[...].astype(F32), (8, ntile)).astype(BF16)
    source = lax.broadcasted_iota(jnp.int32, (ntile, out_rows), 0)
    lane = lax.broadcasted_iota(jnp.int32, (ntile, out_rows), 1)
    lane_source = lax.div(lane, ROWS)
    own_count = jnp.where(source == lane_source, 1.0, 0.0).astype(BF16)
    earlier = jnp.where(source < lane_source, 1.0, 0.0).astype(BF16)
    lane_count = jnp.dot(count, own_count, preferred_element_type=F32)[0:1]
    lane_start = jnp.dot(count, earlier, preferred_element_type=F32)[0:1]
    lane_row = lax.broadcasted_iota(jnp.int32, (1, out_rows), 1)
    lane_rank = lax.rem(lax.div(lane_row, HALF), CAP)
    lane_step = lax.rem(lane_row, HALF)
    slot_row = jnp.where(
        lane_rank < lane_count.astype(jnp.int32),
        (lane_start.astype(jnp.int32) + lane_rank) * HALF + lane_step,
        -1,
    )

    def build_place(b, carry):
        size = cells * HALF // blocks
        base = pl.multiple_of(b * size, size)
        rows = base + lax.broadcasted_iota(jnp.int32, (size, out_rows), 0)
        place[pl.ds(base, size), :] = jnp.where(rows == slot_row, 1.0, 0.0).astype(BF16)
        return carry

    lax.fori_loop(0, blocks, build_place, 0)

    contact = lax.broadcasted_iota(jnp.int32, (chips, cells), 0)
    choose = jnp.concatenate(
        [
            jnp.where(pat_ref[t : t + 1, :] == contact, 1.0, 0.0).astype(BF16)
            for t in (0, 1, 0, 1)
        ],
        axis=1,
    )

    group = ROWS // HALF
    row16 = lax.broadcasted_iota(jnp.int32, (ROWS, seg), 0)
    masks = [
        jnp.where(lax.div(row16, HALF) == n, 1.0, 0.0).astype(BF16)
        for n in range(group)
    ]
    w_copy.wait()
    for c in range(2):
        pltpu.make_async_copy(recv.at[c], recv.at[c], recv_sem.at[1 + c]).wait()
        ordered[...] = (
            jnp.dot(
                place[...],
                recv[c].reshape(out_rows, seg),
                preferred_element_type=F32,
            )
            .astype(BF16)
            .reshape(cells // group, ROWS, seg)
        )

        def read(n, carry, c=c):
            x = ordered[n]
            left_side = jnp.concatenate([x * mask for mask in masks], axis=1)
            right_side = jnp.concatenate(
                [
                    w_ref[pl.ds(n * group, group), t].reshape(group * seg, -1)
                    for t in range(2)
                ],
                axis=1,
            )
            both = jnp.dot(left_side, right_side, preferred_element_type=F32)
            for t in range(2):
                tiles[c, t, pl.ds(pl.multiple_of(n * ROWS, ROWS), ROWS), :] = both[
                    :, t * seg : (t + 1) * seg
                ]
            return carry

        lax.fori_loop(0, cells // group, read, 0, unroll=8)

        for k_in in range(HALF):
            sums = jnp.concatenate(
                [tiles[c, t, pl.ds(k_in, cells, stride=HALF), :] for t in range(2)],
                axis=0,
            )
            high, low = split(sums)
            part[pl.ds(c * HALF + k_in, chips, stride=STEPS), :] = jnp.dot(
                choose,
                jnp.concatenate([high, low], axis=0),
                preferred_element_type=F32,
            )

    partial[...] = part[...].astype(BF16).reshape(chips, STEPS, seg)

    def give(peer_chip):
        pltpu.make_async_remote_copy(
            src_ref=partial.at[peer_chip],
            dst_ref=first.at[chip],
            send_sem=send_sem.at[3],
            recv_sem=recv_sem.at[3],
            device_id=(peer_chip * 2 + core, sec),
            device_id_type=MESH,
        ).start()

    def give_all(base):
        for dz in far + near:
            give(base + at_z[dz])

    along_y(lambda base: (give_all(base), give(base + my_z)))
    give_all(base_y[0])
    pltpu.make_async_copy(partial.at[chip], first.at[chip], recv_sem.at[3]).start()
    pltpu.make_async_copy(first, first, recv_sem.at[3]).wait()
    mine[...] = jnp.sum(first[...].astype(F32), axis=0)

    for step in (2, 1, 3, 0):
        for flip in range(2):
            if step or flip:
                other_sec = lax.rem(sec + step, nsec)
                other_core = lax.rem(core + flip, 2)
                pltpu.make_async_remote_copy(
                    src_ref=mine,
                    dst_ref=second.at[line],
                    send_sem=send_sem.at[4],
                    recv_sem=recv_sem.at[4],
                    device_id=(chip * 2 + other_core, other_sec),
                    device_id_type=MESH,
                ).start()
    pltpu.make_async_copy(mine, second.at[line], recv_sem.at[4]).start()
    pltpu.make_async_copy(second, second, recv_sem.at[4]).wait()
    width = probe_ref.shape[1]
    summed = jnp.sum(second[...], axis=0)
    probe_ref[...] = pltpu.roll(summed, lax.rem(seg - line * width, seg), 1)[:, :width]

    for c in range(2):
        told = ends_in.at[c, pl.ds(0, nsec - 1)]
        pltpu.make_async_copy(told, told, send_sem.at[5 + c]).wait()
        sent = outs.at[c, pl.ds(0, ntile - 1)]
        pltpu.make_async_copy(sent, sent, send_sem.at[1 + c]).wait()
    given = first.at[pl.ds(0, chips - 1)]
    pltpu.make_async_copy(given, given, send_sem.at[3]).wait()
    shared = second.at[pl.ds(0, 2 * nsec - 1)]
    pltpu.make_async_copy(shared, shared, send_sem.at[4]).wait()


def hand_over(fv_ref, probe_ref, fv_out, probe_out):
    fv_out[...] = fv_ref[...]
    probe_out[...] = probe_ref[...]


def on_device(ny, nz, nsec, width, voltage, conductance, reversal, drive, inv_cable, owner_map, peer_counts, pattern, transfer):
    cells, seg = voltage.shape
    chips = ny * nz
    ntile = 2 * chips
    vmem = pl.BlockSpec(memory_space=pltpu.VMEM)
    rows = ntile * ROWS
    results = pl.pallas_call(
        functools.partial(kernel, ny, nz, nsec),
        out_shape=(
            pltpu.VMEM((cells, seg), F32),
            pltpu.VMEM((STEPS, width), F32),
        ),
        in_specs=[pl.BlockSpec(memory_space=pl.ANY)] * 9,
        out_specs=(vmem, vmem),
        scratch_shapes=[
            pltpu.VMEM((cells, seg), F32),
            pltpu.VMEM((cells, seg), F32),
            pltpu.VMEM((cells, seg), F32),
            pltpu.VMEM((STEPS, cells, seg), BF16),
            pltpu.VMEM((seg, seg), F32),
            pltpu.VMEM((1, cells), jnp.int32),
            pltpu.VMEM((1, ntile), jnp.int32),
            pltpu.VMEM((2, cells), jnp.int32),
            pltpu.VMEM(transfer.shape[1:], BF16),
            pltpu.VMEM((STEPS + 1, seg, cells), F32),
            pltpu.VMEM((LAGS, seg, cells), F32),
            pltpu.VMEM((LAGS, seg, cells), F32),
            pltpu.VMEM((2, 6 * HALF, cells), F32),
            pltpu.VMEM((2, 6 * HALF, cells), BF16),
            pltpu.VMEM((2, nsec, 6 * HALF, cells), BF16),
            pltpu.VMEM((2, nsec, 6 * HALF, cells), F32),
            pltpu.VMEM((nsec, 4, 16, cells), F32),
            pltpu.VMEM((nsec, 2, 8, cells), F32),
            pltpu.VMEM((rows, HALF * cells), BF16),
            pltpu.VMEM((cells * HALF, rows), BF16),
            pltpu.VMEM((2, HALF * cells, seg), BF16),
            pltpu.VMEM((2, ntile, ROWS, seg), BF16),
            pltpu.VMEM((2, ntile, ROWS, seg), BF16),
            pltpu.VMEM((cells // 4, ROWS, seg), BF16),
            pltpu.VMEM((2, 2, cells * HALF, seg), F32),
            pltpu.VMEM((chips * STEPS, seg), F32),
            pltpu.VMEM((chips, STEPS, seg), BF16),
            pltpu.VMEM((chips, STEPS, seg), BF16),
            pltpu.VMEM((STEPS, seg), F32),
            pltpu.VMEM((2 * nsec, STEPS, seg), F32),
            pltpu.SemaphoreType.DMA((8,)),
            pltpu.SemaphoreType.DMA,
            pltpu.SemaphoreType.REGULAR((2,)),
            pltpu.SemaphoreType.DMA((7,)),
            pltpu.SemaphoreType.DMA((7,)),
        ],
        compiler_params=pltpu.CompilerParams(
            collective_id=0, has_side_effects=True, vmem_limit_bytes=60 * 1024 * 1024
        ),
        name="cable_probe",
    )(
        voltage,
        conductance,
        reversal,
        drive,
        inv_cable,
        owner_map.reshape(1, -1),
        peer_counts,
        pattern[0].T,
        transfer,
    )
    return pl.pallas_call(
        hand_over,
        out_shape=(
            jax.ShapeDtypeStruct((cells, seg), F32),
            jax.ShapeDtypeStruct((STEPS, width), F32),
        ),
        in_specs=[vmem, vmem],
        out_specs=(vmem, vmem),
        name="hand_over",
    )(*(pltpu.with_memory_space_constraint(x, pltpu.VMEM) for x in results))


def solution(mesh):
    ntile, nsec = mesh.shape["tile"], mesh.shape["sec"]
    chips = ntile // 2
    nz = 8 if chips % 8 == 0 else 2
    ny = chips // nz
    width = chips * 128 // (ntile * nsec)
    placed = (
        P("tile", "sec"),
        P("tile", "sec"),
        P("tile", "sec"),
        P(None, "tile", "sec"),
        P(),
        P("tile"),
        P("tile", None),
        P("sec", "tile", None),
        P("sec", "tile", None, None, None),
    )
    return jax.shard_map(
        functools.partial(on_device, ny, nz, nsec, width),
        mesh=mesh,
        in_specs=placed,
        out_specs=(P("tile", "sec"), P(None, ("tile", "sec"))),
        check_vma=False,
    )
```

```python
import functools

import jax
import jax.numpy as jnp
from jax import lax
from jax.experimental import pallas as pl
from jax.experimental.pallas import tpu as pltpu
from jax.sharding import PartitionSpec as P

MESH = pl.DeviceIdType.MESH
F32 = jnp.float32
BF16 = jnp.bfloat16

STEPS = 8
HALF = 4
CAP = 4
ROWS = CAP * HALF
LAGS = 8
TIME_STEP = 0.25


def far_first(index, count):
    half = lax.div(index + 1, 2)
    return count // 2 + half * (1 - 2 * lax.rem(index, 2))


def split(x):
    high = x.astype(BF16)
    return high, (x - high.astype(F32)).astype(BF16)


def kernel(
    ny,
    nz,
    nsec,
    v_hbm,
    g_hbm,
    e_hbm,
    d_hbm,
    a_hbm,
    own_hbm,
    cnt_hbm,
    pat_hbm,
    w_hbm,
    fv_ref,
    probe_ref,
    v_ref,
    g_ref,
    e_ref,
    d_ref,
    a_ref,
    own_ref,
    cnt_ref,
    pat_ref,
    w_ref,
    zs,
    hl,
    hr,
    ends,
    ends_out,
    ends_in,
    got,
    hpad,
    zpad,
    pick,
    place,
    cur,
    outs,
    recv,
    ordered,
    tiles,
    part,
    partial,
    first,
    mine,
    second,
    in_sem,
    w_sem,
    round_sem,
    send_sem,
    recv_sem,
):
    chips = ny * nz
    ntile = 2 * chips
    cells, seg = v_ref.shape
    tile = lax.axis_index("tile")
    sec = lax.axis_index("sec")
    core = lax.rem(tile, 2)
    chip = lax.div(tile, 2)
    my_y = lax.div(chip, nz)
    my_z = lax.rem(chip, nz)
    line = core * nsec + sec

    base_y = [lax.rem(my_y + dy, ny) * nz for dy in range(ny)]
    at_z = [lax.rem(my_z + dz, nz) for dz in range(nz)]
    y_order = (2, 1, 3)
    far = (4, 3, 5)
    near = (2, 6, 1, 7)

    def along_y(body):
        def step(index, carry):
            body(lax.rem(my_y + far_first(index, ny), ny) * nz)
            return carry

        lax.fori_loop(0, ny - 1, step, 0)

    barrier = pltpu.get_barrier_semaphore()

    def signal(sem, peer, peer_sec):
        pl.semaphore_signal(
            sem, inc=1, device_id=(peer, peer_sec), device_id_type=MESH
        )

    loads = []
    for n, (src, dst) in enumerate(
        (
            (a_hbm, a_ref),
            (g_hbm, g_ref),
            (e_hbm, e_ref),
            (v_hbm, v_ref),
            (d_hbm, d_ref),
            (own_hbm, own_ref),
            (cnt_hbm, cnt_ref),
            (pat_hbm, pat_ref),
        )
    ):
        loads.append(pltpu.make_async_copy(src, dst, in_sem.at[n]))
        loads[-1].start()
    for step in range(1, nsec):
        signal(barrier, tile, lax.rem(sec + step, nsec))
    for dz in (2, nz - 2, 1, nz - 1):
        signal(barrier, (base_y[0] + at_z[dz]) * 2 + core, sec)
    for dy in (2, 1, 3, 0):
        if dy:
            signal(barrier, (base_y[dy] + my_z) * 2 + core, sec)
        signal(barrier, (base_y[dy] + my_z) * 2 + 1 - core, sec)

    for load in loads[:5]:
        load.wait()
    w_copy = pltpu.make_async_copy(w_hbm.at[0], w_ref, w_sem)
    w_copy.start()

    a = a_ref[...]
    a_high, a_low = split(a)
    a_both = jnp.concatenate([a_high, a_low], axis=1)

    def times_cable(x):
        high, low = split(x)
        return jnp.dot(
            a_both, jnp.concatenate([high, high], axis=0), preferred_element_type=F32
        ) + jnp.dot(a_high, low, preferred_element_type=F32)

    gt = g_ref[...].T
    row = lax.broadcasted_iota(jnp.int32, (seg, cells), 0)
    at_end = jnp.where((row == 0) | (row == seg - 1), 0.5, 0.0)
    keep = 1.0 - TIME_STEP * gt - at_end
    leak = gt * e_ref[...].T
    zs[0] = v_ref[...].T
    hl[0] = jnp.broadcast_to(a[:, 0:1] * 0.5, (seg, cells))
    hr[0] = jnp.broadcast_to(a[:, seg - 1 : seg] * 0.5, (seg, cells))

    def advance(k):
        driven = d_ref[k].astype(F32).T
        rhs = keep * zs[k] + TIME_STEP * (leak + driven)
        if k < STEPS - 1:
            after = times_cable(
                jnp.concatenate([rhs, keep * hl[k], keep * hr[k]], axis=1)
            )
            zs[k + 1] = after[:, :cells]
            hl[k + 1] = after[:, cells : 2 * cells]
            hr[k + 1] = after[:, 2 * cells :]
        else:
            zs[k + 1] = times_cable(rhs)

    def offer(c):
        for k in range(HALF):
            at = c * HALF + k
            for n, source in enumerate((zs, hl, hr)):
                ends[c, pl.ds(2 * HALF * n + k, 1), :] = source[at, pl.ds(0, 1), :]
                ends[c, pl.ds(2 * HALF * n + HALF + k, 1), :] = source[
                    at, pl.ds(seg - 1, 1), :
                ]
        ends_out[c] = ends[c].astype(BF16)
        for step in (2, 1, 3):
            pltpu.make_async_remote_copy(
                src_ref=ends_out.at[c],
                dst_ref=ends_in.at[c, sec],
                send_sem=send_sem.at[5 + c],
                recv_sem=recv_sem.at[5 + c],
                device_id=(tile, lax.rem(sec + step, nsec)),
                device_id_type=MESH,
            ).start()
        pltpu.make_async_copy(
            ends_out.at[c], ends_in.at[c, sec], recv_sem.at[5 + c]
        ).start()

    for k in range(HALF - 1):
        advance(k)
    pl.semaphore_wait(barrier, nsec - 1 + 4 + 7)
    offer(0)
    for dy in (2, 1, 3, 0):
        if dy:
            signal(round_sem.at[0], (base_y[dy] + my_z) * 2 + core, sec)
        signal(round_sem.at[0], (base_y[dy] + my_z) * 2 + 1 - core, sec)
    for k in range(HALF - 1, STEPS - 1):
        advance(k)
    offer(1)
    advance(STEPS - 1)
    hpad[:, :, 0:8, :] = jnp.zeros((nsec, 4, 8, cells), F32)

    for load in loads[5:]:
        load.wait()

    own = jnp.broadcast_to(own_ref[...].astype(F32), (cells, cells))
    before = lax.broadcasted_iota(jnp.int32, (cells, cells), 0) < (
        lax.broadcasted_iota(jnp.int32, (cells, cells), 1)
    )
    same = jnp.where(before & (own == own.T), 1.0, 0.0)
    rank = jnp.sum(same, axis=0, keepdims=True)
    placed = own_ref[...] * CAP + rank.astype(jnp.int32)
    blocks = 8
    out_rows = ntile * ROWS
    target = jnp.concatenate([placed * HALF + k for k in range(HALF)], axis=1)

    def build_pick(b, carry):
        size = out_rows // blocks
        base = pl.multiple_of(b * size, size)
        rows = base + lax.broadcasted_iota(jnp.int32, (size, HALF * cells), 0)
        pick[pl.ds(base, size), :] = jnp.where(rows == target, 1.0, 0.0).astype(BF16)
        return carry

    lax.fori_loop(0, blocks, build_pick, 0)

    def meet(c):
        pltpu.make_async_copy(ends_in.at[c], ends_in.at[c], recv_sem.at[5 + c]).wait()
        got[c] = ends_in[c].astype(F32)
        known = (c + 1) * HALF
        for s in range(nsec):
            for q in range(2):
                zpad[s, q, c * HALF : known, :] = got[c, s, q * HALF : (q + 1) * HALF, :]
            for q in range(4):
                hpad[s, q, 8 + c * HALF : 8 + known, :] = got[
                    c, s, (2 + q) * HALF : (3 + q) * HALF, :
                ]
        first_of = [zpad[s, 0, 0:known, :] for s in range(nsec)]
        last_of = [zpad[s, 1, 0:known, :] for s in range(nsec)]
        for j in range(known - 1):
            lasts = [jnp.broadcast_to(x[j : j + 1], (known, cells)) for x in last_of]
            firsts = [jnp.broadcast_to(x[j : j + 1], (known, cells)) for x in first_of]
            for s in range(nsec):
                for q, side in ((0, s - 1), (2, s + 1)):
                    if 0 <= side < nsec:
                        end = lasts[side] if q == 0 else firsts[side]
                        first_of[s] += hpad[s, q, pl.ds(7 - j, known), :] * end
                        last_of[s] += hpad[s, q + 1, pl.ds(7 - j, known), :] * end
        left = jnp.zeros((known, cells), F32)
        right = jnp.zeros((known, cells), F32)
        for s in range(nsec):
            if s > 0:
                left = jnp.where(sec == s, last_of[s - 1], left)
            if s < nsec - 1:
                right = jnp.where(sec == s, first_of[s + 1], right)
        return left, right

    def currents(c):
        left, right = meet(c)
        for k_in in range(HALF):
            k = c * HALF + k_in + 1
            total = zs[k]
            for j in range(k):
                total += (
                    hl[k - 1 - j] * left[j : j + 1] + hr[k - 1 - j] * right[j : j + 1]
                )
            now = total.T
            driven = d_ref[k - 1].astype(F32)
            current = (g_ref[...] * (now - e_ref[...]) - driven).astype(BF16)
            cur[c, k_in * cells : (k_in + 1) * cells, :] = current
            if k == STEPS:
                fv_ref[...] = now

    def pack(c, base):
        size = 2 * nz * ROWS
        rows = pl.ds(pl.multiple_of(base * (2 * ROWS), size), size)
        packed = jnp.dot(pick[rows, :], cur[c], preferred_element_type=F32)
        outs[c, pl.ds(base * 2, 2 * nz)] = packed.astype(BF16).reshape(
            2 * nz, ROWS, seg
        )

    def deliver(c, offsets, fresh):
        def send(peer):
            pltpu.make_async_remote_copy(
                src_ref=outs.at[c, peer],
                dst_ref=recv.at[c, tile],
                send_sem=send_sem.at[1 + c],
                recv_sem=recv_sem.at[1 + c],
                device_id=(peer, sec),
                device_id_type=MESH,
            ).start()

        def send_all(base, at_own_z):
            if fresh:
                pack(c, base)
            for other in (1, 0):
                for dz in offsets:
                    at = (base + at_z[dz]) * 2
                    send(at + 1 - core if other else at + core)
            if at_own_z:
                send((base + my_z) * 2 + 1 - core)
                if at_own_z == 2:
                    send((base + my_z) * 2 + core)

        along_y(lambda base: send_all(base, 2 if offsets is near else 0))
        send_all(base_y[0], 1 if offsets is near else 0)
        if offsets is near:
            pltpu.make_async_copy(
                outs.at[c, tile], recv.at[c, tile], recv_sem.at[1 + c]
            ).start()

    currents(0)
    pl.semaphore_wait(round_sem.at[0], 7)
    for dz in (2, nz - 2):
        signal(round_sem.at[1], (base_y[0] + at_z[dz]) * 2 + core, sec)
    deliver(0, near, True)
    pl.semaphore_wait(round_sem.at[1], 2)
    deliver(0, far, False)
    currents(1)
    deliver(1, far, True)
    deliver(1, near, False)

    count = jnp.broadcast_to(cnt_ref[...].astype(F32), (8, ntile)).astype(BF16)
    source = lax.broadcasted_iota(jnp.int32, (ntile, out_rows), 0)
    lane = lax.broadcasted_iota(jnp.int32, (ntile, out_rows), 1)
    lane_source = lax.div(lane, ROWS)
    own_count = jnp.where(source == lane_source, 1.0, 0.0).astype(BF16)
    earlier = jnp.where(source < lane_source, 1.0, 0.0).astype(BF16)
    lane_count = jnp.dot(count, own_count, preferred_element_type=F32)[0:1]
    lane_start = jnp.dot(count, earlier, preferred_element_type=F32)[0:1]
    lane_row = lax.broadcasted_iota(jnp.int32, (1, out_rows), 1)
    lane_rank = lax.rem(lax.div(lane_row, HALF), CAP)
    lane_step = lax.rem(lane_row, HALF)
    slot_row = jnp.where(
        lane_rank < lane_count.astype(jnp.int32),
        (lane_start.astype(jnp.int32) + lane_rank) * HALF + lane_step,
        -1,
    )

    def build_place(b, carry):
        size = cells * HALF // blocks
        base = pl.multiple_of(b * size, size)
        rows = base + lax.broadcasted_iota(jnp.int32, (size, out_rows), 0)
        place[pl.ds(base, size), :] = jnp.where(rows == slot_row, 1.0, 0.0).astype(BF16)
        return carry

    lax.fori_loop(0, blocks, build_place, 0)

    contact = lax.broadcasted_iota(jnp.int32, (chips, cells), 0)
    choose = jnp.concatenate(
        [
            jnp.where(pat_ref[t : t + 1, :] == contact, 1.0, 0.0).astype(BF16)
            for t in (0, 1, 0, 1)
        ],
        axis=1,
    )

    group = ROWS // HALF
    row16 = lax.broadcasted_iota(jnp.int32, (ROWS, seg), 0)
    masks = [
        jnp.where(lax.div(row16, HALF) == n, 1.0, 0.0).astype(BF16)
        for n in range(group)
    ]
    w_copy.wait()
    for c in range(2):
        pltpu.make_async_copy(recv.at[c], recv.at[c], recv_sem.at[1 + c]).wait()
        ordered[...] = (
            jnp.dot(
                place[...],
                recv[c].reshape(out_rows, seg),
                preferred_element_type=F32,
            )
            .astype(BF16)
            .reshape(cells // group, ROWS, seg)
        )

        def read(n, carry, c=c):
            x = ordered[n]
            left_side = jnp.concatenate([x * mask for mask in masks], axis=1)
            right_side = jnp.concatenate(
                [
                    w_ref[pl.ds(n * group, group), t].reshape(group * seg, -1)
                    for t in range(2)
                ],
                axis=1,
            )
            both = jnp.dot(left_side, right_side, preferred_element_type=F32)
            for t in range(2):
                tiles[c, t, pl.ds(pl.multiple_of(n * ROWS, ROWS), ROWS), :] = both[
                    :, t * seg : (t + 1) * seg
                ]
            return carry

        lax.fori_loop(0, cells // group, read, 0, unroll=16)

        for k_in in range(HALF):
            sums = jnp.concatenate(
                [tiles[c, t, pl.ds(k_in, cells, stride=HALF), :] for t in range(2)],
                axis=0,
            )
            high, low = split(sums)
            part[pl.ds(c * HALF + k_in, chips, stride=STEPS), :] = jnp.dot(
                choose,
                jnp.concatenate([high, low], axis=0),
                preferred_element_type=F32,
            )

    partial[...] = part[...].astype(BF16).reshape(chips, STEPS, seg)

    def give(peer_chip):
        pltpu.make_async_remote_copy(
            src_ref=partial.at[peer_chip],
            dst_ref=first.at[chip],
            send_sem=send_sem.at[3],
            recv_sem=recv_sem.at[3],
            device_id=(peer_chip * 2 + core, sec),
            device_id_type=MESH,
        ).start()

    def give_all(base):
        for dz in far + near:
            give(base + at_z[dz])

    along_y(lambda base: (give_all(base), give(base + my_z)))
    give_all(base_y[0])
    pltpu.make_async_copy(partial.at[chip], first.at[chip], recv_sem.at[3]).start()
    pltpu.make_async_copy(first, first, recv_sem.at[3]).wait()
    mine[...] = jnp.sum(first[...].astype(F32), axis=0)

    for step in (2, 1, 3, 0):
        for flip in range(2):
            if step or flip:
                other_sec = lax.rem(sec + step, nsec)
                other_core = lax.rem(core + flip, 2)
                pltpu.make_async_remote_copy(
                    src_ref=mine,
                    dst_ref=second.at[line],
                    send_sem=send_sem.at[4],
                    recv_sem=recv_sem.at[4],
                    device_id=(chip * 2 + other_core, other_sec),
                    device_id_type=MESH,
                ).start()
    pltpu.make_async_copy(mine, second.at[line], recv_sem.at[4]).start()
    pltpu.make_async_copy(second, second, recv_sem.at[4]).wait()
    width = probe_ref.shape[1]
    summed = jnp.sum(second[...], axis=0)
    probe_ref[...] = pltpu.roll(summed, lax.rem(seg - line * width, seg), 1)[:, :width]

    for c in range(2):
        told = ends_in.at[c, pl.ds(0, nsec - 1)]
        pltpu.make_async_copy(told, told, send_sem.at[5 + c]).wait()
        sent = outs.at[c, pl.ds(0, ntile - 1)]
        pltpu.make_async_copy(sent, sent, send_sem.at[1 + c]).wait()
    given = first.at[pl.ds(0, chips - 1)]
    pltpu.make_async_copy(given, given, send_sem.at[3]).wait()
    shared = second.at[pl.ds(0, 2 * nsec - 1)]
    pltpu.make_async_copy(shared, shared, send_sem.at[4]).wait()


def hand_over(fv_ref, probe_ref, fv_out, probe_out):
    fv_out[...] = fv_ref[...]
    probe_out[...] = probe_ref[...]


def on_device(ny, nz, nsec, width, voltage, conductance, reversal, drive, inv_cable, owner_map, peer_counts, pattern, transfer):
    cells, seg = voltage.shape
    chips = ny * nz
    ntile = 2 * chips
    vmem = pl.BlockSpec(memory_space=pltpu.VMEM)
    rows = ntile * ROWS
    results = pl.pallas_call(
        functools.partial(kernel, ny, nz, nsec),
        out_shape=(
            pltpu.VMEM((cells, seg), F32),
            pltpu.VMEM((STEPS, width), F32),
        ),
        in_specs=[pl.BlockSpec(memory_space=pl.ANY)] * 9,
        out_specs=(vmem, vmem),
        scratch_shapes=[
            pltpu.VMEM((cells, seg), F32),
            pltpu.VMEM((cells, seg), F32),
            pltpu.VMEM((cells, seg), F32),
            pltpu.VMEM((STEPS, cells, seg), BF16),
            pltpu.VMEM((seg, seg), F32),
            pltpu.VMEM((1, cells), jnp.int32),
            pltpu.VMEM((1, ntile), jnp.int32),
            pltpu.VMEM((2, cells), jnp.int32),
            pltpu.VMEM(transfer.shape[1:], BF16),
            pltpu.VMEM((STEPS + 1, seg, cells), F32),
            pltpu.VMEM((LAGS, seg, cells), F32),
            pltpu.VMEM((LAGS, seg, cells), F32),
            pltpu.VMEM((2, 6 * HALF, cells), F32),
            pltpu.VMEM((2, 6 * HALF, cells), BF16),
            pltpu.VMEM((2, nsec, 6 * HALF, cells), BF16),
            pltpu.VMEM((2, nsec, 6 * HALF, cells), F32),
            pltpu.VMEM((nsec, 4, 16, cells), F32),
            pltpu.VMEM((nsec, 2, 8, cells), F32),
            pltpu.VMEM((rows, HALF * cells), BF16),
            pltpu.VMEM((cells * HALF, rows), BF16),
            pltpu.VMEM((2, HALF * cells, seg), BF16),
            pltpu.VMEM((2, ntile, ROWS, seg), BF16),
            pltpu.VMEM((2, ntile, ROWS, seg), BF16),
            pltpu.VMEM((cells // 4, ROWS, seg), BF16),
            pltpu.VMEM((2, 2, cells * HALF, seg), F32),
            pltpu.VMEM((chips * STEPS, seg), F32),
            pltpu.VMEM((chips, STEPS, seg), BF16),
            pltpu.VMEM((chips, STEPS, seg), BF16),
            pltpu.VMEM((STEPS, seg), F32),
            pltpu.VMEM((2 * nsec, STEPS, seg), F32),
            pltpu.SemaphoreType.DMA((8,)),
            pltpu.SemaphoreType.DMA,
            pltpu.SemaphoreType.REGULAR((2,)),
            pltpu.SemaphoreType.DMA((7,)),
            pltpu.SemaphoreType.DMA((7,)),
        ],
        compiler_params=pltpu.CompilerParams(
            collective_id=0, has_side_effects=True, vmem_limit_bytes=60 * 1024 * 1024
        ),
        name="cable_probe",
    )(
        voltage,
        conductance,
        reversal,
        drive,
        inv_cable,
        owner_map.reshape(1, -1),
        peer_counts,
        pattern[0].T,
        transfer,
    )
    return pl.pallas_call(
        hand_over,
        out_shape=(
            jax.ShapeDtypeStruct((cells, seg), F32),
            jax.ShapeDtypeStruct((STEPS, width), F32),
        ),
        in_specs=[vmem, vmem],
        out_specs=(vmem, vmem),
        name="hand_over",
    )(*(pltpu.with_memory_space_constraint(x, pltpu.VMEM) for x in results))


def solution(mesh):
    ntile, nsec = mesh.shape["tile"], mesh.shape["sec"]
    chips = ntile // 2
    nz = 8 if chips % 8 == 0 else 2
    ny = chips // nz
    width = chips * 128 // (ntile * nsec)
    placed = (
        P("tile", "sec"),
        P("tile", "sec"),
        P("tile", "sec"),
        P(None, "tile", "sec"),
        P(),
        P("tile"),
        P("tile", None),
        P("sec", "tile", None),
        P("sec", "tile", None, None, None),
    )
    return jax.shard_map(
        functools.partial(on_device, ny, nz, nsec, width),
        mesh=mesh,
        in_specs=placed,
        out_specs=(P("tile", "sec"), P(None, ("tile", "sec"))),
        check_vma=False,
    )
```

```python
import functools

import jax
import jax.numpy as jnp
from jax import lax
from jax.experimental import pallas as pl
from jax.experimental.pallas import tpu as pltpu
from jax.sharding import PartitionSpec as P

MESH = pl.DeviceIdType.MESH
F32 = jnp.float32
BF16 = jnp.bfloat16

STEPS = 8
HALF = 4
CAP = 4
ROWS = CAP * HALF
LAGS = 8
TIME_STEP = 0.25


def far_first(index, count):
    half = lax.div(index + 1, 2)
    return count // 2 + half * (1 - 2 * lax.rem(index, 2))


def split(x):
    high = x.astype(BF16)
    return high, (x - high.astype(F32)).astype(BF16)


def kernel(
    ny,
    nz,
    nsec,
    v_hbm,
    g_hbm,
    e_hbm,
    d_hbm,
    a_hbm,
    own_hbm,
    cnt_hbm,
    pat_hbm,
    w_hbm,
    fv_ref,
    probe_ref,
    v_ref,
    g_ref,
    e_ref,
    d_ref,
    a_ref,
    own_ref,
    cnt_ref,
    pat_ref,
    w_ref,
    zs,
    hl,
    hr,
    ends,
    ends_out,
    ends_in,
    got,
    hpad,
    zpad,
    pick,
    place,
    cur,
    outs,
    recv,
    ordered,
    tiles,
    part,
    partial,
    first,
    mine,
    second,
    in_sem,
    w_sem,
    round_sem,
    send_sem,
    recv_sem,
):
    chips = ny * nz
    ntile = 2 * chips
    cells, seg = v_ref.shape
    tile = lax.axis_index("tile")
    sec = lax.axis_index("sec")
    core = lax.rem(tile, 2)
    chip = lax.div(tile, 2)
    my_y = lax.div(chip, nz)
    my_z = lax.rem(chip, nz)
    line = core * nsec + sec

    base_y = [lax.rem(my_y + dy, ny) * nz for dy in range(ny)]
    at_z = [lax.rem(my_z + dz, nz) for dz in range(nz)]
    y_order = (2, 1, 3)
    far = (4, 3, 5)
    near = (2, 6, 1, 7)

    def along_y(body):
        def step(index, carry):
            body(lax.rem(my_y + far_first(index, ny), ny) * nz)
            return carry

        lax.fori_loop(0, ny - 1, step, 0)

    barrier = pltpu.get_barrier_semaphore()

    def signal(sem, peer, peer_sec):
        pl.semaphore_signal(
            sem, inc=1, device_id=(peer, peer_sec), device_id_type=MESH
        )

    loads = []
    for n, (src, dst) in enumerate(
        (
            (a_hbm, a_ref),
            (g_hbm, g_ref),
            (e_hbm, e_ref),
            (v_hbm, v_ref),
            (d_hbm, d_ref),
            (own_hbm, own_ref),
            (cnt_hbm, cnt_ref),
            (pat_hbm, pat_ref),
        )
    ):
        loads.append(pltpu.make_async_copy(src, dst, in_sem.at[n]))
        loads[-1].start()
    for step in range(1, nsec):
        signal(barrier, tile, lax.rem(sec + step, nsec))
    for dz in (2, nz - 2, 1, nz - 1):
        signal(barrier, (base_y[0] + at_z[dz]) * 2 + core, sec)
    for dy in (2, 1, 3, 0):
        if dy:
            signal(barrier, (base_y[dy] + my_z) * 2 + core, sec)
        signal(barrier, (base_y[dy] + my_z) * 2 + 1 - core, sec)

    for load in loads[:4]:
        load.wait()

    a = a_ref[...]
    a_high, a_low = split(a)
    a_both = jnp.concatenate([a_high, a_low], axis=1)

    def times_cable(x):
        high, low = split(x)
        return jnp.dot(
            a_both, jnp.concatenate([high, high], axis=0), preferred_element_type=F32
        ) + jnp.dot(a_high, low, preferred_element_type=F32)

    gt = g_ref[...].T
    row = lax.broadcasted_iota(jnp.int32, (seg, cells), 0)
    at_end = jnp.where((row == 0) | (row == seg - 1), 0.5, 0.0)
    keep = 1.0 - TIME_STEP * gt - at_end
    leak = gt * e_ref[...].T
    zs[0] = v_ref[...].T
    hl[0] = jnp.broadcast_to(a[:, 0:1] * 0.5, (seg, cells))
    hr[0] = jnp.broadcast_to(a[:, seg - 1 : seg] * 0.5, (seg, cells))

    def advance(k):
        driven = d_ref[k].astype(F32).T
        rhs = keep * zs[k] + TIME_STEP * (leak + driven)
        if k < STEPS - 1:
            after = times_cable(
                jnp.concatenate([rhs, keep * hl[k], keep * hr[k]], axis=1)
            )
            zs[k + 1] = after[:, :cells]
            hl[k + 1] = after[:, cells : 2 * cells]
            hr[k + 1] = after[:, 2 * cells :]
        else:
            zs[k + 1] = times_cable(rhs)

    def offer(c):
        for k in range(HALF):
            at = c * HALF + k
            for n, source in enumerate((zs, hl, hr)):
                ends[c, pl.ds(2 * HALF * n + k, 1), :] = source[at, pl.ds(0, 1), :]
                ends[c, pl.ds(2 * HALF * n + HALF + k, 1), :] = source[
                    at, pl.ds(seg - 1, 1), :
                ]
        ends_out[c] = ends[c].astype(BF16)
        for step in (2, 1, 3):
            pltpu.make_async_remote_copy(
                src_ref=ends_out.at[c],
                dst_ref=ends_in.at[c, sec],
                send_sem=send_sem.at[5 + c],
                recv_sem=recv_sem.at[5 + c],
                device_id=(tile, lax.rem(sec + step, nsec)),
                device_id_type=MESH,
            ).start()
        pltpu.make_async_copy(
            ends_out.at[c], ends_in.at[c, sec], recv_sem.at[5 + c]
        ).start()

    loads[4].wait()
    w_copy = pltpu.make_async_copy(w_hbm.at[0], w_ref, w_sem)
    w_copy.start()
    for k in range(HALF - 1):
        advance(k)
    pl.semaphore_wait(barrier, nsec - 1 + 4 + 7)
    offer(0)
    for dy in (2, 1, 3, 0):
        if dy:
            signal(round_sem.at[0], (base_y[dy] + my_z) * 2 + core, sec)
        signal(round_sem.at[0], (base_y[dy] + my_z) * 2 + 1 - core, sec)
    for k in range(HALF - 1, STEPS - 1):
        advance(k)
    offer(1)
    advance(STEPS - 1)
    hpad[:, :, 0:8, :] = jnp.zeros((nsec, 4, 8, cells), F32)

    for load in loads[5:]:
        load.wait()

    own = jnp.broadcast_to(own_ref[...].astype(F32), (cells, cells))
    before = lax.broadcasted_iota(jnp.int32, (cells, cells), 0) < (
        lax.broadcasted_iota(jnp.int32, (cells, cells), 1)
    )
    same = jnp.where(before & (own == own.T), 1.0, 0.0)
    rank = jnp.sum(same, axis=0, keepdims=True)
    placed = own_ref[...] * CAP + rank.astype(jnp.int32)
    blocks = 8
    out_rows = ntile * ROWS
    target = jnp.concatenate([placed * HALF + k for k in range(HALF)], axis=1)

    def build_pick(b, carry):
        size = out_rows // blocks
        base = pl.multiple_of(b * size, size)
        rows = base + lax.broadcasted_iota(jnp.int32, (size, HALF * cells), 0)
        pick[pl.ds(base, size), :] = jnp.where(rows == target, 1.0, 0.0).astype(BF16)
        return carry

    lax.fori_loop(0, blocks, build_pick, 0)

    def meet(c):
        pltpu.make_async_copy(ends_in.at[c], ends_in.at[c], recv_sem.at[5 + c]).wait()
        got[c] = ends_in[c].astype(F32)
        known = (c + 1) * HALF
        for s in range(nsec):
            for q in range(2):
                zpad[s, q, c * HALF : known, :] = got[c, s, q * HALF : (q + 1) * HALF, :]
            for q in range(4):
                hpad[s, q, 8 + c * HALF : 8 + known, :] = got[
                    c, s, (2 + q) * HALF : (3 + q) * HALF, :
                ]
        first_of = [zpad[s, 0, 0:known, :] for s in range(nsec)]
        last_of = [zpad[s, 1, 0:known, :] for s in range(nsec)]
        for j in range(known - 1):
            lasts = [jnp.broadcast_to(x[j : j + 1], (known, cells)) for x in last_of]
            firsts = [jnp.broadcast_to(x[j : j + 1], (known, cells)) for x in first_of]
            for s in range(nsec):
                for q, side in ((0, s - 1), (2, s + 1)):
                    if 0 <= side < nsec:
                        end = lasts[side] if q == 0 else firsts[side]
                        first_of[s] += hpad[s, q, pl.ds(7 - j, known), :] * end
                        last_of[s] += hpad[s, q + 1, pl.ds(7 - j, known), :] * end
        left = jnp.zeros((known, cells), F32)
        right = jnp.zeros((known, cells), F32)
        for s in range(nsec):
            if s > 0:
                left = jnp.where(sec == s, last_of[s - 1], left)
            if s < nsec - 1:
                right = jnp.where(sec == s, first_of[s + 1], right)
        return left, right

    def currents(c):
        left, right = meet(c)
        for k_in in range(HALF):
            k = c * HALF + k_in + 1
            total = zs[k]
            for j in range(k):
                total += (
                    hl[k - 1 - j] * left[j : j + 1] + hr[k - 1 - j] * right[j : j + 1]
                )
            now = total.T
            driven = d_ref[k - 1].astype(F32)
            current = (g_ref[...] * (now - e_ref[...]) - driven).astype(BF16)
            cur[c, k_in * cells : (k_in + 1) * cells, :] = current
            if k == STEPS:
                fv_ref[...] = now

    def pack(c, base):
        size = 2 * nz * ROWS
        rows = pl.ds(pl.multiple_of(base * (2 * ROWS), size), size)
        packed = jnp.dot(pick[rows, :], cur[c], preferred_element_type=F32)
        outs[c, pl.ds(base * 2, 2 * nz)] = packed.astype(BF16).reshape(
            2 * nz, ROWS, seg
        )

    def deliver(c, offsets, fresh):
        def send(peer):
            pltpu.make_async_remote_copy(
                src_ref=outs.at[c, peer],
                dst_ref=recv.at[c, tile],
                send_sem=send_sem.at[1 + c],
                recv_sem=recv_sem.at[1 + c],
                device_id=(peer, sec),
                device_id_type=MESH,
            ).start()

        def send_all(base, at_own_z):
            if fresh:
                pack(c, base)
            for other in (1, 0):
                for dz in offsets:
                    at = (base + at_z[dz]) * 2
                    send(at + 1 - core if other else at + core)
            if at_own_z:
                send((base + my_z) * 2 + 1 - core)
                if at_own_z == 2:
                    send((base + my_z) * 2 + core)

        along_y(lambda base: send_all(base, 2 if offsets is near else 0))
        send_all(base_y[0], 1 if offsets is near else 0)
        if offsets is near:
            pltpu.make_async_copy(
                outs.at[c, tile], recv.at[c, tile], recv_sem.at[1 + c]
            ).start()

    currents(0)
    pl.semaphore_wait(round_sem.at[0], 7)
    for dz in (2, nz - 2):
        signal(round_sem.at[1], (base_y[0] + at_z[dz]) * 2 + core, sec)
    deliver(0, near, True)
    pl.semaphore_wait(round_sem.at[1], 2)
    deliver(0, far, False)
    currents(1)
    deliver(1, far, True)
    deliver(1, near, False)

    count = jnp.broadcast_to(cnt_ref[...].astype(F32), (8, ntile)).astype(BF16)
    source = lax.broadcasted_iota(jnp.int32, (ntile, out_rows), 0)
    lane = lax.broadcasted_iota(jnp.int32, (ntile, out_rows), 1)
    lane_source = lax.div(lane, ROWS)
    own_count = jnp.where(source == lane_source, 1.0, 0.0).astype(BF16)
    earlier = jnp.where(source < lane_source, 1.0, 0.0).astype(BF16)
    lane_count = jnp.dot(count, own_count, preferred_element_type=F32)[0:1]
    lane_start = jnp.dot(count, earlier, preferred_element_type=F32)[0:1]
    lane_row = lax.broadcasted_iota(jnp.int32, (1, out_rows), 1)
    lane_rank = lax.rem(lax.div(lane_row, HALF), CAP)
    lane_step = lax.rem(lane_row, HALF)
    slot_row = jnp.where(
        lane_rank < lane_count.astype(jnp.int32),
        (lane_start.astype(jnp.int32) + lane_rank) * HALF + lane_step,
        -1,
    )

    def build_place(b, carry):
        size = cells * HALF // blocks
        base = pl.multiple_of(b * size, size)
        rows = base + lax.broadcasted_iota(jnp.int32, (size, out_rows), 0)
        place[pl.ds(base, size), :] = jnp.where(rows == slot_row, 1.0, 0.0).astype(BF16)
        return carry

    lax.fori_loop(0, blocks, build_place, 0)

    contact = lax.broadcasted_iota(jnp.int32, (chips, cells), 0)
    choose = jnp.concatenate(
        [
            jnp.where(pat_ref[t : t + 1, :] == contact, 1.0, 0.0).astype(BF16)
            for t in (0, 1, 0, 1)
        ],
        axis=1,
    )

    group = ROWS // HALF
    row16 = lax.broadcasted_iota(jnp.int32, (ROWS, seg), 0)
    masks = [
        jnp.where(lax.div(row16, HALF) == n, 1.0, 0.0).astype(BF16)
        for n in range(group)
    ]
    w_copy.wait()
    for c in range(2):
        pltpu.make_async_copy(recv.at[c], recv.at[c], recv_sem.at[1 + c]).wait()
        ordered[...] = (
            jnp.dot(
                place[...],
                recv[c].reshape(out_rows, seg),
                preferred_element_type=F32,
            )
            .astype(BF16)
            .reshape(cells // group, ROWS, seg)
        )

        def read(n, carry, c=c):
            x = ordered[n]
            left_side = jnp.concatenate([x * mask for mask in masks], axis=1)
            right_side = jnp.concatenate(
                [
                    w_ref[pl.ds(n * group, group), t].reshape(group * seg, -1)
                    for t in range(2)
                ],
                axis=1,
            )
            both = jnp.dot(left_side, right_side, preferred_element_type=F32)
            for t in range(2):
                tiles[c, t, pl.ds(pl.multiple_of(n * ROWS, ROWS), ROWS), :] = both[
                    :, t * seg : (t + 1) * seg
                ]
            return carry

        lax.fori_loop(0, cells // group, read, 0, unroll=16)

        for k_in in range(HALF):
            sums = jnp.concatenate(
                [tiles[c, t, pl.ds(k_in, cells, stride=HALF), :] for t in range(2)],
                axis=0,
            )
            high, low = split(sums)
            part[pl.ds(c * HALF + k_in, chips, stride=STEPS), :] = jnp.dot(
                choose,
                jnp.concatenate([high, low], axis=0),
                preferred_element_type=F32,
            )

    partial[...] = part[...].astype(BF16).reshape(chips, STEPS, seg)

    def give(peer_chip):
        pltpu.make_async_remote_copy(
            src_ref=partial.at[peer_chip],
            dst_ref=first.at[chip],
            send_sem=send_sem.at[3],
            recv_sem=recv_sem.at[3],
            device_id=(peer_chip * 2 + core, sec),
            device_id_type=MESH,
        ).start()

    def give_all(base):
        for dz in far + near:
            give(base + at_z[dz])

    along_y(lambda base: (give_all(base), give(base + my_z)))
    give_all(base_y[0])
    pltpu.make_async_copy(partial.at[chip], first.at[chip], recv_sem.at[3]).start()
    pltpu.make_async_copy(first, first, recv_sem.at[3]).wait()
    mine[...] = jnp.sum(first[...].astype(F32), axis=0)

    for step in (2, 1, 3, 0):
        for flip in range(2):
            if step or flip:
                other_sec = lax.rem(sec + step, nsec)
                other_core = lax.rem(core + flip, 2)
                pltpu.make_async_remote_copy(
                    src_ref=mine,
                    dst_ref=second.at[line],
                    send_sem=send_sem.at[4],
                    recv_sem=recv_sem.at[4],
                    device_id=(chip * 2 + other_core, other_sec),
                    device_id_type=MESH,
                ).start()
    pltpu.make_async_copy(mine, second.at[line], recv_sem.at[4]).start()
    pltpu.make_async_copy(second, second, recv_sem.at[4]).wait()
    width = probe_ref.shape[1]
    summed = jnp.sum(second[...], axis=0)
    probe_ref[...] = pltpu.roll(summed, lax.rem(seg - line * width, seg), 1)[:, :width]

    for c in range(2):
        told = ends_in.at[c, pl.ds(0, nsec - 1)]
        pltpu.make_async_copy(told, told, send_sem.at[5 + c]).wait()
        sent = outs.at[c, pl.ds(0, ntile - 1)]
        pltpu.make_async_copy(sent, sent, send_sem.at[1 + c]).wait()
    given = first.at[pl.ds(0, chips - 1)]
    pltpu.make_async_copy(given, given, send_sem.at[3]).wait()
    shared = second.at[pl.ds(0, 2 * nsec - 1)]
    pltpu.make_async_copy(shared, shared, send_sem.at[4]).wait()


def hand_over(fv_ref, probe_ref, fv_out, probe_out):
    fv_out[...] = fv_ref[...]
    probe_out[...] = probe_ref[...]


def on_device(ny, nz, nsec, width, voltage, conductance, reversal, drive, inv_cable, owner_map, peer_counts, pattern, transfer):
    cells, seg = voltage.shape
    chips = ny * nz
    ntile = 2 * chips
    vmem = pl.BlockSpec(memory_space=pltpu.VMEM)
    rows = ntile * ROWS
    results = pl.pallas_call(
        functools.partial(kernel, ny, nz, nsec),
        out_shape=(
            pltpu.VMEM((cells, seg), F32),
            pltpu.VMEM((STEPS, width), F32),
        ),
        in_specs=[pl.BlockSpec(memory_space=pl.ANY)] * 9,
        out_specs=(vmem, vmem),
        scratch_shapes=[
            pltpu.VMEM((cells, seg), F32),
            pltpu.VMEM((cells, seg), F32),
            pltpu.VMEM((cells, seg), F32),
            pltpu.VMEM((STEPS, cells, seg), BF16),
            pltpu.VMEM((seg, seg), F32),
            pltpu.VMEM((1, cells), jnp.int32),
            pltpu.VMEM((1, ntile), jnp.int32),
            pltpu.VMEM((2, cells), jnp.int32),
            pltpu.VMEM(transfer.shape[1:], BF16),
            pltpu.VMEM((STEPS + 1, seg, cells), F32),
            pltpu.VMEM((LAGS, seg, cells), F32),
            pltpu.VMEM((LAGS, seg, cells), F32),
            pltpu.VMEM((2, 6 * HALF, cells), F32),
            pltpu.VMEM((2, 6 * HALF, cells), BF16),
            pltpu.VMEM((2, nsec, 6 * HALF, cells), BF16),
            pltpu.VMEM((2, nsec, 6 * HALF, cells), F32),
            pltpu.VMEM((nsec, 4, 16, cells), F32),
            pltpu.VMEM((nsec, 2, 8, cells), F32),
            pltpu.VMEM((rows, HALF * cells), BF16),
            pltpu.VMEM((cells * HALF, rows), BF16),
            pltpu.VMEM((2, HALF * cells, seg), BF16),
            pltpu.VMEM((2, ntile, ROWS, seg), BF16),
            pltpu.VMEM((2, ntile, ROWS, seg), BF16),
            pltpu.VMEM((cells // 4, ROWS, seg), BF16),
            pltpu.VMEM((2, 2, cells * HALF, seg), F32),
            pltpu.VMEM((chips * STEPS, seg), F32),
            pltpu.VMEM((chips, STEPS, seg), BF16),
            pltpu.VMEM((chips, STEPS, seg), BF16),
            pltpu.VMEM((STEPS, seg), F32),
            pltpu.VMEM((2 * nsec, STEPS, seg), F32),
            pltpu.SemaphoreType.DMA((8,)),
            pltpu.SemaphoreType.DMA,
            pltpu.SemaphoreType.REGULAR((2,)),
            pltpu.SemaphoreType.DMA((7,)),
            pltpu.SemaphoreType.DMA((7,)),
        ],
        compiler_params=pltpu.CompilerParams(
            collective_id=0, has_side_effects=True, vmem_limit_bytes=60 * 1024 * 1024
        ),
        name="cable_probe",
    )(
        voltage,
        conductance,
        reversal,
        drive,
        inv_cable,
        owner_map.reshape(1, -1),
        peer_counts,
        pattern[0].T,
        transfer,
    )
    return pl.pallas_call(
        hand_over,
        out_shape=(
            jax.ShapeDtypeStruct((cells, seg), F32),
            jax.ShapeDtypeStruct((STEPS, width), F32),
        ),
        in_specs=[vmem, vmem],
        out_specs=(vmem, vmem),
        name="hand_over",
    )(*(pltpu.with_memory_space_constraint(x, pltpu.VMEM) for x in results))


def solution(mesh):
    ntile, nsec = mesh.shape["tile"], mesh.shape["sec"]
    chips = ntile // 2
    nz = 8 if chips % 8 == 0 else 2
    ny = chips // nz
    width = chips * 128 // (ntile * nsec)
    placed = (
        P("tile", "sec"),
        P("tile", "sec"),
        P("tile", "sec"),
        P(None, "tile", "sec"),
        P(),
        P("tile"),
        P("tile", None),
        P("sec", "tile", None),
        P("sec", "tile", None, None, None),
    )
    return jax.shard_map(
        functools.partial(on_device, ny, nz, nsec, width),
        mesh=mesh,
        in_specs=placed,
        out_specs=(P("tile", "sec"), P(None, ("tile", "sec"))),
        check_vma=False,
    )
```
